32 devices in a mesh: col: 8 (over z, y), row: 4 (over x, core).
Axes of the slice: x: 2, y: 2, z: 4, core: 2. Of those that a mesh axis runs over, the one named last changes fastest.
Arguments:
- sigma_anc: float32 [16, 16, 128, 128], P('row', 'col'), as said below
- panel_u: float32 [8, 8, 128, 128], P('col'), may hold values from -0.1875 to 0.1875
- structure: int32 [8, 8], P('col'), may hold values from 0 to 15, as said below
- diag_inv: float32 [8, 128, 128], P('col'), may hold values from -0.5 to 0.5
Outputs:
- panel_out: float32 [8, 16, 128, 128], P('col', 'row')
- diag_out: float32 [8, 128, 128], P('col')
The draws below stay inside these ranges and needn't reach their ends.
Inputs may be any that keep to these rules, and one draw needn't show every extreme that they name: `structure`: each row holds 8 different ancestor numbers in increasing order. `sigma_anc`: the matrix is symmetric: block (a, b) is the transpose of block (b, a).
All inputs are finite; a program needn't handle non-finite values.
Results may differ from the reference program's by a relative error of at most 0.0003.
Values sent between devices are 32-bit elements; how exact they have to be, the bound alone decides.
A program may use at most 128 MiB of HBM per device.

```python
import jax
import jax.numpy as jnp
from jax import lax

B = 128
NA = 16
K = 8
NS = 8


def draw_sigma_anc(key, part):
    side = NA * B
    base = jax.random.normal(jax.random.fold_in(key, 11), (side, side), jnp.float32)
    full = (base + base.T) * 0.7
    return full.reshape(NA, B, NA, B).transpose(0, 2, 1, 3)


def draw_structure(key, part):
    keys = jax.random.split(jax.random.fold_in(key, 17), NS)
    perms = jax.vmap(lambda k: jax.random.permutation(k, NA))(keys).astype(jnp.int32)
    chosen = perms[:, :K]
    inner = 1 + jax.random.permutation(jax.random.fold_in(key, 19), NA - 2)[:K - 2].astype(jnp.int32)
    first = jnp.concatenate([jnp.array([0, NA - 1], jnp.int32), inner])
    chosen = chosen.at[0].set(first)
    return jnp.sort(chosen, axis=1).astype(jnp.int32)


def block_levels(rng, dims, shards, low, high):
    gain, own = 1.0, jax.random.fold_in(rng, 6)
    for axis_at, blocks in shards:
        steps = jnp.exp(jax.random.uniform(jax.random.fold_in(own, axis_at), (blocks,), jnp.float32, low / len(shards), high / len(shards)))
        gain = gain * jnp.repeat(steps, dims[axis_at] // blocks).reshape([-1 if axis == axis_at else 1 for axis in range(len(dims))])
    return gain


def centred(key, shape, width, most, cuts=(), kind=jnp.bfloat16):
    level = block_levels(key, shape, cuts, -0.22, 0.18) if cuts else 1.0
    drawn = jax.random.normal(key, shape, jnp.float32) * width * level
    return jnp.minimum(jnp.maximum(drawn, -most), most).astype(kind)


def setup_inputs(seed: int = 0) -> dict:
    key_of = jax.random.split(jax.random.key(seed), 5)
    sigma_anc = draw_sigma_anc(jax.random.fold_in(key_of[4], 71), 0)
    panel_u = centred(key_of[1], (NS, K, B, B), (K * B) ** -0.5, 0.1875, ((0, 8),), jnp.float32)
    structure = draw_structure(jax.random.fold_in(key_of[4], 71), 0)
    diag_inv = centred(key_of[3], (NS, B, B), B ** -0.5, 0.5, ((0, 8),), jnp.float32)
    return dict(sigma_anc=sigma_anc, panel_u=panel_u, structure=structure, diag_inv=diag_inv)


def reference(sigma_anc, panel_u, structure, diag_inv):
    whole = sigma_anc.transpose(0, 2, 1, 3).reshape(NA * B, NA * B)
    offsets = jnp.arange(B, dtype=jnp.int32)
    ancestors = jnp.arange(NA, dtype=jnp.int32)

    def one_node(items):
        blocks, picks, inverse = items
        columns = (picks[:, None] * B + offsets[None, :]).reshape(-1).astype(jnp.int32)
        chosen = jnp.take(whole, columns, axis=1)
        stacked = blocks.reshape(K * B, B)
        result = jnp.dot(chosen, stacked, precision=lax.Precision.HIGHEST, preferred_element_type=jnp.float32)
        member = jnp.any(picks[None, :] == ancestors[:, None], axis=1).astype(jnp.float32)
        panel = -result.reshape(NA, B, B) * member[:, None, None]
        onehot = (picks[:, None] == ancestors[None, :]).astype(jnp.float32)
        dense = jnp.einsum("ka,kxy->axy", onehot, blocks, precision=lax.Precision.HIGHEST)
        update = jnp.dot(dense.reshape(NA * B, B).T, panel.reshape(NA * B, B), precision=lax.Precision.HIGHEST, preferred_element_type=jnp.float32)
        base = jnp.dot(inverse.T, inverse, precision=lax.Precision.HIGHEST, preferred_element_type=jnp.float32)
        return panel, base - update

    panel_out, diag_out = lax.map(one_node, (panel_u, structure, diag_inv))
    return panel_out, diag_out
```

```python
import functools

import jax
import jax.numpy as jnp
from jax import lax
from jax.experimental import pallas as pl
from jax.experimental.pallas import tpu as pltpu
from jax.sharding import PartitionSpec as P

MESH = pl.DeviceIdType.MESH
HIGHEST = lax.Precision.HIGHEST


def split(x):
    high = x.astype(jnp.bfloat16)
    return high, (x - high.astype(jnp.float32)).astype(jnp.bfloat16)


def dot(a, b):
    return jnp.dot(a, b, preferred_element_type=jnp.float32)


def dot_t(a, b):
    return lax.dot_general(
        a, b, (((0,), (0,)), ((), ())), precision=HIGHEST, preferred_element_type=jnp.float32
    )


def bend(plane):
    return lax.rem((plane + 1) // 2, 2)


def kernel(
    planes,
    rows,
    chunks,
    sigma_ref,
    u_ref,
    s_ref,
    inv_ref,
    panel_ref,
    diag_ref,
    raw,
    st_hi,
    st_lo,
    ubuf,
    sbuf,
    yout,
    yin,
    share,
    shares,
    x_send,
    c_send,
    s_recv,
    u_send,
    u_recv,
    n_send,
    n_recv,
    y_send,
    y_recv,
    d_send,
    d_recv,
):
    row_count, col_count, width = sigma_ref.shape[0], sigma_ref.shape[1], sigma_ref.shape[2]
    cols, entries, nodes = 2 * planes, u_ref.shape[1], ubuf.shape[0]
    half = rows // 2
    span = entries // chunks
    per_row = row_count // col_count
    col, row = lax.axis_index("col"), lax.axis_index("row")
    z, y = col // 2, lax.rem(col, 2)
    mate = row + 1 - 2 * lax.rem(row, 2)
    up, down, side = col + 2, col - 2, col + 1 - 2 * y

    def node(m):
        plane = m * half + lax.rem(row, half)
        return plane, lax.rem(row // half + bend(plane), 2)

    def node_col(m):
        plane, lane = node(m)
        return plane * 2 + lane

    own_row = lax.rem(y + bend(z), 2) * half + lax.rem(z, half)
    own_slot = z // half
    is_source = own_row == row

    def dev(c, r=None):
        return {"col": c, "row": row if r is None else r}

    barrier = pltpu.get_barrier_semaphore()

    def greet(where):
        pl.semaphore_signal(barrier, inc=1, device_id=where, device_id_type=MESH)

    def number(flag):
        return flag.astype(jnp.int32)

    @pl.when(z < planes - 1)
    def _():
        greet(dev(up))

    @pl.when(z > 0)
    def _():
        greet(dev(down))

    greet(dev(side))
    for o in range(1, rows):
        greet(dev(col, lax.rem(row + o, rows)))
    expected = number(z < planes - 1) + number(z > 0) + 1 + rows - 1
    expected += jnp.where(is_source, cols - 1, 0)
    home = col // per_row

    @pl.loop(0, nodes)
    def _(m):
        @pl.when(node_col(m) != col)
        def _():
            greet(dev(node_col(m)))

    def self_out(m):
        return jnp.logical_and(node_col(m) == col, home == row)

    for i in range(per_row):

        @pl.when(jnp.logical_or(row * per_row + i != col, own_row != row))
        def _():
            greet(dev(row * per_row + i, own_row))

    expected += nodes - number(jnp.logical_and(is_source, home == row))

    def member(b):
        found, where = jnp.int32(0), jnp.int32(0)
        for k in range(entries):
            hit = s_ref[0, k] == b
            found, where = jnp.where(hit, 1, found), jnp.where(hit, k, where)
        return found.astype(jnp.float32), where

    pl.semaphore_wait(barrier, expected)

    def u_copies(m, n, source_ref):
        plane, lane = node(m)
        mine = y == lane
        rng = pl.ds(n * span, span)

        def to(way, c):
            return pltpu.make_async_remote_copy(
                source_ref.at[rng], ubuf.at[m, rng], u_send.at[way, m, n], u_recv.at[m, n], dev(c), MESH
            )

        return (
            (jnp.logical_and(mine, jnp.logical_and(z >= plane, z < planes - 1)), to(0, up)),
            (jnp.logical_and(mine, jnp.logical_and(z <= plane, z > 0)), to(1, down)),
            (mine, to(2, side)),
        )

    def u_start(m, n, source_ref):
        for flag, copy in u_copies(m, n, source_ref):
            pl.when(flag)(copy.start)

    def u_arrival(m, n):
        mine = ubuf.at[m, pl.ds(n * span, span)]
        return pltpu.make_async_remote_copy(
            mine, mine, u_send.at[0, m, n], u_recv.at[m, n], dev(side), MESH
        )

    def n_copy(o):
        return pltpu.make_async_remote_copy(
            s_ref,
            sbuf.at[pl.ds(own_slot, 1)],
            n_send.at[o - 1],
            n_recv.at[own_slot],
            dev(lax.rem(col + o, cols)),
            MESH,
        )

    def n_arrival(m):
        mine = sbuf.at[pl.ds(m, 1)]
        return pltpu.make_async_remote_copy(
            mine, mine, n_send.at[0], n_recv.at[m], dev(side), MESH
        )

    def x_copy(o, a):
        return pltpu.make_async_remote_copy(
            sigma_ref.at[a],
            raw.at[row, a],
            x_send.at[o, a],
            s_recv.at[row, a],
            dev(col, lax.rem(row + 2 * o, rows)),
            MESH,
        )

    def own_copy(a):
        return pltpu.make_async_remote_copy(
            sigma_ref.at[a], raw.at[row, a], c_send.at[0, a], s_recv.at[row, a], dev(col, mate), MESH
        )

    def c_copy(o, a):
        r = lax.rem(row + 2 * o, rows)
        return pltpu.make_async_remote_copy(
            raw.at[r, a], raw.at[r, a], c_send.at[o, a], s_recv.at[r, a], dev(col, mate), MESH
        )

    def s_arrival(r, a):
        return pltpu.make_async_remote_copy(
            raw.at[r, a], raw.at[r, a], c_send.at[0, a], s_recv.at[r, a], dev(col, mate), MESH
        )

    @pl.when(is_source)
    def _():
        for o in range(1, cols):
            n_copy(o).start()

        @pl.loop(0, chunks)
        def _(n):
            u_start(own_slot, n, u_ref.at[0])

    for a in range(row_count):
        for o in range(1, half):
            x_copy(o, a).start()
    for a in range(row_count):
        own_copy(a).start()

    def keep(r, a, source):
        for i in range(col_count):
            high, low = split(source[i].T)
            st_hi[r * row_count + a, i * width : (i + 1) * width] = high
            st_lo[r * row_count + a, i * width : (i + 1) * width] = low

    @pl.when(is_source)
    def _():
        ubuf[own_slot] = u_ref[0]
        for k in range(entries):
            sbuf[own_slot, k] = s_ref[0, k]

    for a in range(row_count):
        keep(row, a, sigma_ref.at[a])
    inv = inv_ref[0]
    diag_ref[0] = dot_t(inv, inv)

    def s_forward(a):
        for o in range(1, half):
            r = lax.rem(row + 2 * o, rows)
            s_arrival(r, a).wait_recv()
            c_copy(o, a).start()
            keep(r, a, raw.at[r, a])

    def distance(m):
        plane, lane = node(m)
        return jnp.abs(z - plane) + jnp.where(y == lane, 0, 1)

    steps = chunks + 2 * planes

    @pl.loop(0, max(steps, 2 * row_count))
    def _(t):
        @pl.loop(0, nodes)
        def _(m):
            n = t - 2 * (distance(m) - 1)

            @pl.when(jnp.logical_and(jnp.logical_and(n >= 0, n < chunks), node_col(m) != col))
            def _():
                u_arrival(m, n).wait_recv()
                u_start(m, n, ubuf.at[m])

        @pl.when(jnp.logical_and(lax.rem(t, 2) == 1, t < 2 * row_count))
        def _():
            s_forward(t // 2)

    for o in range(half):
        r = lax.rem(mate + 2 * o, rows)
        for a in range(row_count):
            s_arrival(r, a).wait_recv()
            keep(r, a, raw.at[r, a])

    def y_copy(m):
        return pltpu.make_async_remote_copy(
            yout.at[m],
            yin.at[pl.ds(lax.rem(col, per_row) * col_count, col_count)],
            y_send.at[m],
            y_recv.at[lax.rem(col, per_row)],
            dev(node_col(m), home),
            MESH,
        )

    def y_arrival(i):
        mine = yin.at[pl.ds(i * col_count, col_count)]
        return pltpu.make_async_remote_copy(
            mine, mine, y_send.at[0], y_recv.at[i], dev(row * per_row + i, own_row), MESH
        )

    @pl.loop(0, nodes)
    def _(m):
        @pl.when(node_col(m) != col)
        def _():
            n_arrival(m).wait_recv()

        def term(k, total):
            b = sbuf[m, k]
            high, low = split(ubuf[m, k])
            both = dot(st_hi[b], jnp.concatenate([high, low], axis=1))
            return total + (both[:, :width] + (both[:, width:] + dot(st_lo[b], high)))

        total = lax.fori_loop(
            0, entries, term, jnp.zeros((col_count * width, width), jnp.float32), unroll=min(entries, 8)
        )
        for i in range(col_count):
            yout[m, i] = total[i * width : (i + 1) * width]

        @pl.when(jnp.logical_not(self_out(m)))
        def _():
            y_copy(m).start()

        @pl.when(self_out(m))
        def _():
            yin[pl.ds(lax.rem(col, per_row) * col_count, col_count)] = yout[m]

    row_start = row * row_count
    total = jnp.zeros((width, width), jnp.float32)
    for i in range(per_row):

        @pl.when(jnp.logical_or(row * per_row + i != col, own_row != row))
        def _():
            y_arrival(i).wait_recv()

        for q in range(col_count):
            a = i * col_count + q
            found, where = member(row_start + a)
            panel = -yin[a] * found
            panel_ref[0, a] = panel
            total += dot_t(u_ref[0, where] * found, panel)
    share[...] = total

    def d_copy(o):
        return pltpu.make_async_remote_copy(
            share,
            shares.at[o - 1],
            d_send.at[o - 1],
            d_recv.at[o - 1],
            dev(col, lax.rem(row + o, rows)),
            MESH,
        )

    for o in range(1, rows):
        d_copy(o).start()
    diag_ref[0] -= total
    for o in range(1, rows):
        d_copy(o).wait_recv()
        diag_ref[0] -= shares[o - 1]

    for o in range(1, rows):
        d_copy(o).wait_send()
    for a in range(row_count):
        own_copy(a).wait_send()
        for o in range(1, half):
            x_copy(o, a).wait_send()
            c_copy(o, a).wait_send()

    @pl.when(is_source)
    def _():
        for o in range(1, cols):
            n_copy(o).wait_send()

    @pl.loop(0, nodes)
    def _(m):
        @pl.when(jnp.logical_not(self_out(m)))
        def _():
            y_copy(m).wait_send()

        @pl.loop(0, chunks)
        def _(n):
            for flag, copy in u_copies(m, n, ubuf.at[m]):
                pl.when(flag)(copy.wait_send)


def local(sigma_anc, panel_u, structure, diag_inv):
    row_count, col_count, width = sigma_anc.shape[0], sigma_anc.shape[1], sigma_anc.shape[2]
    entries = panel_u.shape[1]
    cols, rows = lax.axis_size("col"), lax.axis_size("row")
    planes, nodes, half = cols // 2, cols // rows, rows // 2
    ancestors = rows * row_count
    chunks = next(c for c in (4, 2, 1) if entries % c == 0)
    block = (width, width)
    f32, bf16 = jnp.float32, jnp.bfloat16
    vmem = pl.BlockSpec(memory_space=pltpu.VMEM)
    dma = pltpu.SemaphoreType.DMA
    return pl.pallas_call(
        functools.partial(kernel, planes, rows, chunks),
        out_shape=(
            jax.ShapeDtypeStruct((1, row_count, *block), f32),
            jax.ShapeDtypeStruct((1, *block), f32),
        ),
        in_specs=[vmem, vmem, pl.BlockSpec(memory_space=pltpu.SMEM), vmem],
        out_specs=(vmem, vmem),
        scratch_shapes=[
            pltpu.VMEM((rows, row_count, col_count, *block), f32),
            pltpu.VMEM((ancestors, col_count * width, width), bf16),
            pltpu.VMEM((ancestors, col_count * width, width), bf16),
            pltpu.VMEM((nodes, entries, *block), f32),
            pltpu.SMEM((nodes, entries), jnp.int32),
            pltpu.VMEM((nodes, col_count, *block), f32),
            pltpu.VMEM((row_count, *block), f32),
            pltpu.VMEM(block, f32),
            pltpu.VMEM((rows - 1, *block), f32),
            dma((half, row_count)),
            dma((half, row_count)),
            dma((rows, row_count)),
            dma((3, nodes, chunks)),
            dma((nodes, chunks)),
            dma((cols - 1,)),
            dma((nodes,)),
            dma((nodes,)),
            dma((row_count // col_count,)),
            dma((rows - 1,)),
            dma((rows - 1,)),
        ],
        compiler_params=pltpu.CompilerParams(
            collective_id=0, has_side_effects=True, vmem_limit_bytes=60 * 1024 * 1024
        ),
    )(sigma_anc, panel_u, structure, diag_inv)


def solution(mesh):
    placed = (
        P("row", "col", None, None),
        P("col", None, None, None),
        P("col", None),
        P("col", None, None),
    )
    return jax.shard_map(
        local,
        mesh=mesh,
        in_specs=placed,
        out_specs=(P("col", "row", None, None), P("col", None, None)),
        check_vma=False,
    )
```

```python
import functools

import jax
import jax.numpy as jnp
from jax import lax
from jax.experimental import pallas as pl
from jax.experimental.pallas import tpu as pltpu
from jax.sharding import PartitionSpec as P

MESH = pl.DeviceIdType.MESH
HIGHEST = lax.Precision.HIGHEST


def split(x):
    high = x.astype(jnp.bfloat16)
    return high, (x - high.astype(jnp.float32)).astype(jnp.bfloat16)


def dot(a, b):
    return jnp.dot(a, b, preferred_element_type=jnp.float32)


def dot_t(a, b):
    return lax.dot_general(
        a, b, (((0,), (0,)), ((), ())), precision=HIGHEST, preferred_element_type=jnp.float32
    )


def kernel(
    planes,
    rows,
    sigma_ref,
    u_ref,
    s_ref,
    inv_ref,
    panel_ref,
    diag_ref,
    raw,
    st_hi,
    st_lo,
    uown,
    iown,
    ubuf,
    sbuf,
    wt_hi,
    wt_lo,
    yout,
    yin,
    share,
    shares,
    x_send,
    c_send,
    s_recv,
    a_send,
    a_recv,
    b_send,
    b_recv,
    n_send,
    n_recv,
    y_send,
    y_recv,
    d_send,
    d_recv,
    load,
):
    row_count, col_count, width = sigma_ref.shape[0], sigma_ref.shape[1], sigma_ref.shape[2]
    entries, groups = u_ref.shape[1], planes // rows
    half = rows // 2
    per_row = row_count // col_count
    col, row = lax.axis_index("col"), lax.axis_index("row")
    z, y = col // 2, lax.rem(col, 2)
    core = lax.rem(row, 2)
    mate, side = row + 1 - 2 * core, col + 1 - 2 * y

    def dev(c, r=None):
        return {"col": c, "row": row if r is None else r}

    twist = lax.rem(row // half + y, 2)

    def partner(i, e):
        s = 2 * core + jnp.where(e == 0, twist, 1 - twist)
        return rows * i + lax.rem(s - z + planes, rows)

    def node_col(i, e):
        return partner(i, e) * 2 + jnp.where(e == 0, y, 1 - y)

    def worker(other):
        return half * lax.rem(y + z + other, 2) + lax.rem((z + other) // 2, 2)

    home = col // per_row
    slot = z // rows

    barrier = pltpu.get_barrier_semaphore()

    def greet(where):
        pl.semaphore_signal(barrier, inc=1, device_id=where, device_id_type=MESH)

    local_sigma = pltpu.make_async_copy(sigma_ref, raw.at[row], load.at[0])
    local_u = pltpu.make_async_copy(u_ref.at[0], uown, load.at[1])
    local_inv = pltpu.make_async_copy(inv_ref.at[0], iown, load.at[2])
    expected = jnp.int32(rows)
    greet(dev(side))
    for o in range(1, rows):
        greet(dev(col, lax.rem(row + o, rows)))
    for i in range(groups):
        away = partner(i, 0) != z
        pl.when(away)(lambda: greet(dev(node_col(i, 0))))
        expected += away.astype(jnp.int32)
    local_u.start()
    local_sigma.start()
    local_inv.start()
    pl.semaphore_wait(barrier, expected)

    def a_copy(i, n):
        return pltpu.make_async_remote_copy(
            u_ref.at[0, n], ubuf.at[0, slot, n], a_send.at[i, n], a_recv.at[slot, n], dev(node_col(i, 0)), MESH
        )

    def a_arrival(i, n):
        mine = ubuf.at[0, i, n]
        return pltpu.make_async_remote_copy(mine, mine, a_send.at[i, n], a_recv.at[i, n], dev(side), MESH)

    def b_copy(i, n, source):
        return pltpu.make_async_remote_copy(
            source, ubuf.at[1, i, n], b_send.at[i, n], b_recv.at[i, n], dev(side), MESH
        )

    def n_copy(e, i, source):
        at = slot if e == 0 else i
        where = node_col(i, 0) if e == 0 else side
        return pltpu.make_async_remote_copy(
            source, sbuf.at[pl.ds(e * groups + at, 1)], n_send.at[e, i], n_recv.at[e, at], dev(where), MESH
        )

    def n_arrival(e, i):
        mine = sbuf.at[pl.ds(e * groups + i, 1)]
        return pltpu.make_async_remote_copy(mine, mine, n_send.at[e, i], n_recv.at[e, i], dev(side), MESH)

    def x_copy(o, a):
        return pltpu.make_async_remote_copy(
            sigma_ref.at[a],
            raw.at[row, a],
            x_send.at[o, a],
            s_recv.at[row, a],
            dev(col, lax.rem(row + 2 * o, rows)),
            MESH,
        )

    def own_copy(a):
        return pltpu.make_async_remote_copy(
            sigma_ref.at[a], raw.at[row, a], c_send.at[0, a], s_recv.at[row, a], dev(col, mate), MESH
        )

    def c_copy(o, a):
        r = lax.rem(row + 2 * o, rows)
        return pltpu.make_async_remote_copy(
            raw.at[r, a], raw.at[r, a], c_send.at[o, a], s_recv.at[r, a], dev(col, mate), MESH
        )

    def s_arrival(r, a):
        return pltpu.make_async_remote_copy(
            raw.at[r, a], raw.at[r, a], c_send.at[0, a], s_recv.at[r, a], dev(col, mate), MESH
        )

    for i in range(groups):
        away = partner(i, 0) != z

        @pl.when(away)
        def _():
            n_copy(0, i, s_ref).start()

        @pl.when(jnp.logical_not(away))
        def _():
            n_copy(1, i, s_ref).start()

        @pl.loop(0, entries)
        def _(n):
            @pl.when(away)
            def _():
                a_copy(i, n).start()

            @pl.when(jnp.logical_not(away))
            def _():
                b_copy(i, n, u_ref.at[0, n]).start()

    for a in range(row_count):
        for o in range(1, half):
            x_copy(o, a).start()
    for a in range(row_count):
        own_copy(a).start()

    def member(b):
        found, where = jnp.int32(0), jnp.int32(0)
        for k in range(entries):
            hit = s_ref[0, k] == b
            found, where = jnp.where(hit, 1, found), jnp.where(hit, k, where)
        return found.astype(jnp.float32), where

    def keep(r, a):
        for i in range(col_count):
            high, low = split(raw[r, a, i].T)
            st_hi[r * row_count + a, i * width : (i + 1) * width] = high
            st_lo[r * row_count + a, i * width : (i + 1) * width] = low

    local_u.wait()
    row_start = row * row_count
    found = []
    for a in range(row_count):
        here, where = member(row_start + a)
        found.append(here)
        high, low = split((uown[where] * here).T)
        lanes = slice(a % col_count * width, (a % col_count + 1) * width)
        wt_hi[a // col_count, :, lanes] = high
        wt_lo[a // col_count, :, lanes] = low

    for i in range(groups):

        @pl.when(partner(i, 0) == z)
        def _():
            ubuf[0, i] = uown[...]
            for k in range(entries):
                sbuf[i, k] = s_ref[0, k]

    local_sigma.wait()
    for a in range(row_count):
        keep(row, a)
    local_inv.wait()
    inv = iown[...]
    diag_ref[0] = dot_t(inv, inv)

    def s_forward(a):
        for o in range(1, half):
            r = lax.rem(row + 2 * o, rows)
            s_arrival(r, a).wait_recv()
            c_copy(o, a).start()
            keep(r, a)

    @pl.loop(0, entries)
    def _(n):
        for i in range(groups):

            @pl.when(partner(i, 0) != z)
            def _():
                @pl.when(n == 0)
                def _():
                    n_arrival(0, i).wait_recv()
                    n_copy(1, i, sbuf.at[pl.ds(i, 1)]).start()

                a_arrival(i, n).wait_recv()
                b_copy(i, n, ubuf.at[0, i, n]).start()

        for a in range(row_count):
            pl.when(n == (a + 1) * entries // row_count - 1)(functools.partial(s_forward, a))

    for o in range(half):
        r = lax.rem(mate + 2 * o, rows)
        for a in range(row_count):
            s_arrival(r, a).wait_recv()
            keep(r, a)

    def self_out(i, e):
        return jnp.logical_and(node_col(i, e) == col, home == row)

    def y_copy(i, e):
        return pltpu.make_async_remote_copy(
            yout.at[e, i],
            yin.at[pl.ds(lax.rem(col, per_row) * col_count, col_count)],
            y_send.at[e, i],
            y_recv.at[lax.rem(col, per_row)],
            dev(node_col(i, e), home),
            MESH,
        )

    def y_from(i):
        return row * per_row + i

    def y_arrival(i):
        mine = yin.at[pl.ds(i * col_count, col_count)]
        return pltpu.make_async_remote_copy(
            mine, mine, y_send.at[0, 0], y_recv.at[i], dev(side), MESH
        )

    @pl.loop(0, 2 * groups)
    def _(m):
        e, i = m // groups, lax.rem(m, groups)

        @pl.when(e == 1)
        def _():
            n_arrival(1, i).wait_recv()
            for n in range(entries):
                mine = ubuf.at[1, i, n]
                pltpu.make_async_remote_copy(
                    mine, mine, b_send.at[i, n], b_recv.at[i, n], dev(side), MESH
                ).wait_recv()

        def term(k, total):
            b = sbuf[m, k]
            high, low = split(ubuf[e, i, k])
            both = dot(st_hi[b], jnp.concatenate([high, low], axis=1))
            return total + (both[:, :width] + (both[:, width:] + dot(st_lo[b], high)))

        total = lax.fori_loop(
            0, entries, term, jnp.zeros((col_count * width, width), jnp.float32), unroll=min(entries, 8)
        )
        for q in range(col_count):
            yout[e, i, q] = total[q * width : (q + 1) * width]

        @pl.when(jnp.logical_not(self_out(i, e)))
        def _():
            y_copy(i, e).start()

        @pl.when(self_out(i, e))
        def _():
            yin[pl.ds(lax.rem(col, per_row) * col_count, col_count)] = yout[e, i]

    total = jnp.zeros((width, width), jnp.float32)
    for i in range(per_row):
        other = y_from(i)

        @pl.when(jnp.logical_or(other != col, worker(other // 2) != row))
        def _():
            y_arrival(i).wait_recv()

        panels = []
        for q in range(col_count):
            a = i * col_count + q
            panels.append(-yin[a] * found[a])
            panel_ref[0, a] = panels[q]
        high, low = split(jnp.concatenate(panels, axis=0))
        both = dot(wt_hi[i], jnp.concatenate([high, low], axis=1))
        total += both[:, :width] + (both[:, width:] + dot(wt_lo[i], high))
    share[0] = total

    def pair_copy():
        return pltpu.make_async_remote_copy(
            share.at[0], shares.at[0], d_send.at[0], d_recv.at[0], dev(col, mate), MESH
        )

    def chip_copy(o):
        return pltpu.make_async_remote_copy(
            share.at[1],
            shares.at[o],
            d_send.at[o],
            d_recv.at[o],
            dev(col, lax.rem(row + 2 * o, rows)),
            MESH,
        )

    pair_copy().start()
    pair_copy().wait_recv()
    total += shares[0]
    share[1] = total
    for o in range(1, half):
        chip_copy(o).start()

    pair_copy().wait_send()
    for a in range(row_count):
        own_copy(a).wait_send()
        for o in range(1, half):
            x_copy(o, a).wait_send()
            c_copy(o, a).wait_send()
    for i in range(groups):
        away = partner(i, 0) != z
        pl.when(away)(n_copy(0, i, s_ref).wait_send)
        n_copy(1, i, s_ref).wait_send()
        for e in range(2):
            pl.when(jnp.logical_not(self_out(i, e)))(y_copy(i, e).wait_send)

        @pl.loop(0, entries)
        def _(n):
            pl.when(away)(a_copy(i, n).wait_send)
            b_copy(i, n, u_ref.at[0, n]).wait_send()

    for o in range(1, half):
        chip_copy(o).wait_recv()
        total += shares[o]
    diag_ref[0] -= total
    for o in range(1, half):
        chip_copy(o).wait_send()


def local(sigma_anc, panel_u, structure, diag_inv):
    row_count, col_count, width = sigma_anc.shape[0], sigma_anc.shape[1], sigma_anc.shape[2]
    entries = panel_u.shape[1]
    cols, rows = lax.axis_size("col"), lax.axis_size("row")
    planes, half = cols // 2, rows // 2
    groups = planes // rows
    per_row = row_count // col_count
    ancestors = rows * row_count
    block = (width, width)
    f32, bf16 = jnp.float32, jnp.bfloat16
    vmem, hbm = pl.BlockSpec(memory_space=pltpu.VMEM), pl.BlockSpec(memory_space=pl.ANY)
    dma = pltpu.SemaphoreType.DMA
    return pl.pallas_call(
        functools.partial(kernel, planes, rows),
        out_shape=(
            jax.ShapeDtypeStruct((1, row_count, *block), f32),
            jax.ShapeDtypeStruct((1, *block), f32),
        ),
        in_specs=[hbm, hbm, pl.BlockSpec(memory_space=pltpu.SMEM), hbm],
        out_specs=(vmem, vmem),
        scratch_shapes=[
            pltpu.VMEM((rows, row_count, col_count, *block), f32),
            pltpu.VMEM((ancestors, col_count * width, width), bf16),
            pltpu.VMEM((ancestors, col_count * width, width), bf16),
            pltpu.VMEM((entries, *block), f32),
            pltpu.VMEM(block, f32),
            pltpu.VMEM((2, groups, entries, *block), f32),
            pltpu.SMEM((2 * groups, entries), jnp.int32),
            pltpu.VMEM((per_row, width, col_count * width), bf16),
            pltpu.VMEM((per_row, width, col_count * width), bf16),
            pltpu.VMEM((2, groups, col_count, *block), f32),
            pltpu.VMEM((row_count, *block), f32),
            pltpu.VMEM((2, *block), f32),
            pltpu.VMEM((half, *block), f32),
            dma((half, row_count)),
            dma((half, row_count)),
            dma((rows, row_count)),
            dma((groups, entries)),
            dma((groups, entries)),
            dma((groups, entries)),
            dma((groups, entries)),
            dma((2, groups)),
            dma((2, groups)),
            dma((2, groups)),
            dma((per_row,)),
            dma((half,)),
            dma((half,)),
            dma((3,)),
        ],
        compiler_params=pltpu.CompilerParams(
            collective_id=0, has_side_effects=True, vmem_limit_bytes=60 * 1024 * 1024
        ),
    )(sigma_anc, panel_u, structure, diag_inv)


def solution(mesh):
    placed = (
        P("row", "col", None, None),
        P("col", None, None, None),
        P("col", None),
        P("col", None, None),
    )
    return jax.shard_map(
        local,
        mesh=mesh,
        in_specs=placed,
        out_specs=(P("col", "row", None, None), P("col", None, None)),
        check_vma=False,
    )
```

```python
import functools

import jax
import jax.numpy as jnp
from jax import lax
from jax.experimental import pallas as pl
from jax.experimental.pallas import tpu as pltpu
from jax.sharding import PartitionSpec as P

MESH = pl.DeviceIdType.MESH
HIGHEST = lax.Precision.HIGHEST


def split(x):
    high = x.astype(jnp.bfloat16)
    return high, (x - high.astype(jnp.float32)).astype(jnp.bfloat16)


def dot(a, b):
    return jnp.dot(a, b, preferred_element_type=jnp.float32)


def dot_t(a, b):
    return lax.dot_general(
        a, b, (((0,), (0,)), ((), ())), precision=HIGHEST, preferred_element_type=jnp.float32
    )


def kernel(
    planes,
    rows,
    sigma_ref,
    u_ref,
    s_ref,
    inv_ref,
    panel_ref,
    diag_ref,
    raw,
    st_hi,
    st_lo,
    uown,
    iown,
    ubuf,
    sbuf,
    wt_hi,
    wt_lo,
    yout,
    yin,
    share,
    shares,
    x_send,
    c_send,
    s_recv,
    a_send,
    a_recv,
    b_send,
    b_recv,
    n_send,
    n_recv,
    y_send,
    y_recv,
    d_send,
    d_recv,
    load,
):
    row_count, col_count, width = sigma_ref.shape[0], sigma_ref.shape[1], sigma_ref.shape[2]
    entries, groups = u_ref.shape[1], planes // rows
    half = rows // 2
    per_row = row_count // col_count
    col, row = lax.axis_index("col"), lax.axis_index("row")
    z, y = col // 2, lax.rem(col, 2)
    core = lax.rem(row, 2)
    mate, side = row + 1 - 2 * core, col + 1 - 2 * y

    def dev(c, r=None):
        return {"col": c, "row": row if r is None else r}

    twist = lax.rem(row // half + y, 2)

    def partner(i, e):
        s = 2 * core + jnp.where(e == 0, twist, 1 - twist)
        return rows * i + lax.rem(s - z + planes, rows)

    def node_col(i, e):
        return partner(i, e) * 2 + jnp.where(e == 0, y, 1 - y)

    def worker(other):
        return half * lax.rem(y + z + other, 2) + lax.rem((z + other) // 2, 2)

    home = col // per_row
    slot = z // rows

    barrier = pltpu.get_barrier_semaphore()

    def greet(where):
        pl.semaphore_signal(barrier, inc=1, device_id=where, device_id_type=MESH)

    local_sigma = pltpu.make_async_copy(sigma_ref, raw.at[row], load.at[0])
    local_u = pltpu.make_async_copy(u_ref.at[0], uown, load.at[1])
    local_inv = pltpu.make_async_copy(inv_ref.at[0], iown, load.at[2])
    expected = jnp.int32(rows)
    greet(dev(side))
    for o in range(1, rows):
        greet(dev(col, lax.rem(row + o, rows)))
    for i in range(groups):
        away = partner(i, 0) != z
        pl.when(away)(lambda: greet(dev(node_col(i, 0))))
        expected += away.astype(jnp.int32)
    local_u.start()
    local_sigma.start()
    local_inv.start()
    pl.semaphore_wait(barrier, expected)

    def a_copy(i, n):
        return pltpu.make_async_remote_copy(
            u_ref.at[0, n], ubuf.at[0, slot, n], a_send.at[i, n], a_recv.at[slot, n], dev(node_col(i, 0)), MESH
        )

    def a_arrival(i, n):
        mine = ubuf.at[0, i, n]
        return pltpu.make_async_remote_copy(mine, mine, a_send.at[i, n], a_recv.at[i, n], dev(side), MESH)

    def b_copy(i, n, source):
        return pltpu.make_async_remote_copy(
            source, ubuf.at[1, i, n], b_send.at[i, n], b_recv.at[i, n], dev(side), MESH
        )

    def n_copy(e, i, source):
        at = slot if e == 0 else i
        where = node_col(i, 0) if e == 0 else side
        return pltpu.make_async_remote_copy(
            source, sbuf.at[pl.ds(e * groups + at, 1)], n_send.at[e, i], n_recv.at[e, at], dev(where), MESH
        )

    def n_arrival(e, i):
        mine = sbuf.at[pl.ds(e * groups + i, 1)]
        return pltpu.make_async_remote_copy(mine, mine, n_send.at[e, i], n_recv.at[e, i], dev(side), MESH)

    def x_copy(o, a):
        return pltpu.make_async_remote_copy(
            sigma_ref.at[a],
            raw.at[row, a],
            x_send.at[o, a],
            s_recv.at[row, a],
            dev(col, lax.rem(row + 2 * o, rows)),
            MESH,
        )

    def own_copy(a):
        return pltpu.make_async_remote_copy(
            sigma_ref.at[a], raw.at[row, a], c_send.at[0, a], s_recv.at[row, a], dev(col, mate), MESH
        )

    def c_copy(o, a):
        r = lax.rem(row + 2 * o, rows)
        return pltpu.make_async_remote_copy(
            raw.at[r, a], raw.at[r, a], c_send.at[o, a], s_recv.at[r, a], dev(col, mate), MESH
        )

    def s_arrival(r, a):
        return pltpu.make_async_remote_copy(
            raw.at[r, a], raw.at[r, a], c_send.at[0, a], s_recv.at[r, a], dev(col, mate), MESH
        )

    for i in range(groups):
        away = partner(i, 0) != z

        @pl.when(away)
        def _():
            n_copy(0, i, s_ref).start()

        @pl.when(jnp.logical_not(away))
        def _():
            n_copy(1, i, s_ref).start()

        @pl.loop(0, entries)
        def _(n):
            @pl.when(away)
            def _():
                a_copy(i, n).start()

            @pl.when(jnp.logical_not(away))
            def _():
                b_copy(i, n, u_ref.at[0, n]).start()

    for a in range(row_count):
        for o in range(1, half):
            x_copy(o, a).start()
    for a in range(row_count):
        own_copy(a).start()

    def member(b):
        found, where = jnp.int32(0), jnp.int32(0)
        for k in range(entries):
            hit = s_ref[0, k] == b
            found, where = jnp.where(hit, 1, found), jnp.where(hit, k, where)
        return found.astype(jnp.float32), where

    def keep(r, a):
        for i in range(col_count):
            high, low = split(raw[r, a, i].T)
            st_hi[r * row_count + a, i * width : (i + 1) * width] = high
            st_lo[r * row_count + a, i * width : (i + 1) * width] = low

    local_u.wait()
    row_start = row * row_count
    found = []
    for a in range(row_count):
        here, where = member(row_start + a)
        found.append(here)
        high, low = split((uown[where] * here).T)
        lanes = slice(a % col_count * width, (a % col_count + 1) * width)
        wt_hi[a // col_count, :, lanes] = high
        wt_lo[a // col_count, :, lanes] = low

    for i in range(groups):

        @pl.when(partner(i, 0) == z)
        def _():
            ubuf[0, i] = uown[...]
            for k in range(entries):
                sbuf[i, k] = s_ref[0, k]

    local_sigma.wait()
    for a in range(row_count):
        keep(row, a)
    local_inv.wait()
    inv = iown[...]
    diag_ref[0] = dot_t(inv, inv)

    def s_forward(a):
        for o in range(1, half):
            r = lax.rem(row + 2 * o, rows)
            s_arrival(r, a).wait_recv()
            c_copy(o, a).start()
            keep(r, a)

    @pl.loop(0, entries)
    def _(n):
        for i in range(groups):

            @pl.when(partner(i, 0) != z)
            def _():
                @pl.when(n == 0)
                def _():
                    n_arrival(0, i).wait_recv()
                    n_copy(1, i, sbuf.at[pl.ds(i, 1)]).start()

                a_arrival(i, n).wait_recv()
                b_copy(i, n, ubuf.at[0, i, n]).start()

        for a in range(row_count):
            pl.when(n == (a + 1) * entries // row_count - 1)(functools.partial(s_forward, a))

    for o in range(half):
        r = lax.rem(mate + 2 * o, rows)
        for a in range(row_count):
            s_arrival(r, a).wait_recv()
            keep(r, a)

    def self_out(i, e):
        return jnp.logical_and(node_col(i, e) == col, home == row)

    def y_copy(i, e):
        return pltpu.make_async_remote_copy(
            yout.at[e, i],
            yin.at[pl.ds(lax.rem(col, per_row) * col_count, col_count)],
            y_send.at[e, i],
            y_recv.at[lax.rem(col, per_row)],
            dev(node_col(i, e), home),
            MESH,
        )

    def y_from(i):
        return row * per_row + i

    def y_arrival(i):
        mine = yin.at[pl.ds(i * col_count, col_count)]
        return pltpu.make_async_remote_copy(
            mine, mine, y_send.at[0, 0], y_recv.at[i], dev(side), MESH
        )

    @pl.loop(0, 2 * groups)
    def _(m):
        e, i = m // groups, lax.rem(m, groups)

        @pl.when(e == 1)
        def _():
            n_arrival(1, i).wait_recv()
            for n in range(entries):
                mine = ubuf.at[1, i, n]
                pltpu.make_async_remote_copy(
                    mine, mine, b_send.at[i, n], b_recv.at[i, n], dev(side), MESH
                ).wait_recv()

        def term(k, total):
            b = sbuf[m, k]
            high, low = split(ubuf[e, i, k])
            both = dot(st_hi[b], jnp.concatenate([high, low], axis=1))
            return total + (both[:, :width] + (both[:, width:] + dot(st_lo[b], high)))

        total = lax.fori_loop(
            0, entries, term, jnp.zeros((col_count * width, width), jnp.float32), unroll=min(entries, 8)
        )
        for q in range(col_count):
            yout[e, i, q] = total[q * width : (q + 1) * width]

        @pl.when(jnp.logical_not(self_out(i, e)))
        def _():
            y_copy(i, e).start()

        @pl.when(self_out(i, e))
        def _():
            yin[pl.ds(lax.rem(col, per_row) * col_count, col_count)] = yout[e, i]

    total = jnp.zeros((width, width), jnp.float32)
    for i in range(per_row):
        other = y_from(i)

        @pl.when(jnp.logical_or(other != col, worker(other // 2) != row))
        def _():
            y_arrival(i).wait_recv()

        panels = []
        for q in range(col_count):
            a = i * col_count + q
            panels.append(-yin[a] * found[a])
            panel_ref[0, a] = panels[q]
        high, low = split(jnp.concatenate(panels, axis=0))
        both = dot(wt_hi[i], jnp.concatenate([high, low], axis=1))
        total += both[:, :width] + (both[:, width:] + dot(wt_lo[i], high))
    share[0] = total

    def pair_copy():
        return pltpu.make_async_remote_copy(
            share.at[0], shares.at[0], d_send.at[0], d_recv.at[0], dev(col, mate), MESH
        )

    def chip_copy(o):
        return pltpu.make_async_remote_copy(
            share.at[1],
            shares.at[o],
            d_send.at[o],
            d_recv.at[o],
            dev(col, lax.rem(row + 2 * o, rows)),
            MESH,
        )

    pair_copy().start()
    pair_copy().wait_recv()
    total += shares[0]
    share[1] = total
    for o in range(1, half):
        chip_copy(o).start()

    pair_copy().wait_send()
    for a in range(row_count):
        own_copy(a).wait_send()
        for o in range(1, half):
            x_copy(o, a).wait_send()
            c_copy(o, a).wait_send()
    for i in range(groups):
        away = partner(i, 0) != z
        pl.when(away)(n_copy(0, i, s_ref).wait_send)
        n_copy(1, i, s_ref).wait_send()
        for e in range(2):
            pl.when(jnp.logical_not(self_out(i, e)))(y_copy(i, e).wait_send)

        @pl.loop(0, entries)
        def _(n):
            pl.when(away)(a_copy(i, n).wait_send)
            b_copy(i, n, u_ref.at[0, n]).wait_send()

    for o in range(1, half):
        chip_copy(o).wait_recv()
        total += shares[o]
    diag_ref[0] -= total
    for o in range(1, half):
        chip_copy(o).wait_send()


def local(sigma_anc, panel_u, structure, diag_inv):
    row_count, col_count, width = sigma_anc.shape[0], sigma_anc.shape[1], sigma_anc.shape[2]
    entries = panel_u.shape[1]
    cols, rows = lax.axis_size("col"), lax.axis_size("row")
    planes, half = cols // 2, rows // 2
    groups = planes // rows
    per_row = row_count // col_count
    ancestors = rows * row_count
    block = (width, width)
    f32, bf16 = jnp.float32, jnp.bfloat16
    vmem, hbm = pl.BlockSpec(memory_space=pltpu.VMEM), pl.BlockSpec(memory_space=pl.ANY)
    dma = pltpu.SemaphoreType.DMA
    return pl.pallas_call(
        functools.partial(kernel, planes, rows),
        out_shape=(
            jax.ShapeDtypeStruct((1, row_count, *block), f32),
            jax.ShapeDtypeStruct((1, *block), f32),
        ),
        in_specs=[hbm, hbm, pl.BlockSpec(memory_space=pltpu.SMEM), hbm],
        out_specs=(vmem, vmem),
        scratch_shapes=[
            pltpu.VMEM((rows, row_count, col_count, *block), f32),
            pltpu.VMEM((ancestors, col_count * width, width), bf16),
            pltpu.VMEM((ancestors, col_count * width, width), bf16),
            pltpu.VMEM((entries, *block), f32),
            pltpu.VMEM(block, f32),
            pltpu.VMEM((2, groups, entries, *block), f32),
            pltpu.SMEM((2 * groups, entries), jnp.int32),
            pltpu.VMEM((per_row, width, col_count * width), bf16),
            pltpu.VMEM((per_row, width, col_count * width), bf16),
            pltpu.VMEM((2, groups, col_count, *block), f32),
            pltpu.VMEM((row_count, *block), f32),
            pltpu.VMEM((2, *block), f32),
            pltpu.VMEM((half, *block), f32),
            dma((half, row_count)),
            dma((half, row_count)),
            dma((rows, row_count)),
            dma((groups, entries)),
            dma((groups, entries)),
            dma((groups, entries)),
            dma((groups, entries)),
            dma((2, groups)),
            dma((2, groups)),
            dma((2, groups)),
            dma((per_row,)),
            dma((half,)),
            dma((half,)),
            dma((3,)),
        ],
        compiler_params=pltpu.CompilerParams(
            collective_id=0, has_side_effects=True, vmem_limit_bytes=48 * 1024 * 1024
        ),
    )(*(pltpu.with_memory_space_constraint(v, pltpu.HBM) for v in (sigma_anc, panel_u, structure, diag_inv)))


def solution(mesh):
    placed = (
        P("row", "col", None, None),
        P("col", None, None, None),
        P("col", None),
        P("col", None, None),
    )
    return jax.shard_map(
        local,
        mesh=mesh,
        in_specs=placed,
        out_specs=(P("col", "row", None, None), P("col", None, None)),
        check_vma=False,
    )
```

```python
import functools

import jax
import jax.numpy as jnp
from jax import lax
from jax.experimental import pallas as pl
from jax.experimental.pallas import tpu as pltpu
from jax.sharding import PartitionSpec as P

MESH = pl.DeviceIdType.MESH
HIGHEST = lax.Precision.HIGHEST
LAG = 3


def split(x):
    high = x.astype(jnp.bfloat16)
    return high, (x - high.astype(jnp.float32)).astype(jnp.bfloat16)


def dot(a, b):
    return jnp.dot(a, b, preferred_element_type=jnp.float32)


def dot_t(a, b):
    return lax.dot_general(
        a, b, (((0,), (0,)), ((), ())), precision=HIGHEST, preferred_element_type=jnp.float32
    )


def bend(plane):
    return lax.rem((plane + 1) // 2, 2)


def kernel(
    planes,
    rows,
    sigma_ref,
    u_ref,
    s_ref,
    inv_ref,
    panel_ref,
    diag_ref,
    own,
    raw,
    st_hi,
    st_lo,
    uown,
    iown,
    ubuf,
    sbuf,
    wt_hi,
    wt_lo,
    yout,
    yin,
    share,
    shares,
    x_send,
    c_send,
    s_recv,
    a_send,
    o_send,
    a_recv,
    b_send,
    b_recv,
    n_send,
    n_recv,
    y_send,
    y_recv,
    d_send,
    d_recv,
    load,
):
    row_count, col_count, width = sigma_ref.shape[0], sigma_ref.shape[1], sigma_ref.shape[2]
    entries, groups = u_ref.shape[1], planes // rows
    half = rows // 2
    pack = 2 - entries % 2
    per_row = row_count // col_count
    col, row = lax.axis_index("col"), lax.axis_index("row")
    z, y = col // 2, lax.rem(col, 2)
    core = lax.rem(row, 2)
    mate, side = row + 1 - 2 * core, col + 1 - 2 * y

    def dev(c, r=None):
        return {"col": c, "row": row if r is None else r}

    depth = planes // 2
    upper = z // depth
    even = lax.rem(row // half + upper + y + 1, 2)

    def plane_of(i, e):
        odd = jnp.where(e == 0, even, 1 - even)
        return rows * i + jnp.where(core == 0, 3 * odd, 2 - odd)

    def node_col(i, e):
        return plane_of(i, e) * 2 + jnp.where(e == 0, y, 1 - y)

    def worker(other):
        return half * lax.rem(y + z + other // depth + 1, 2) + bend(z)

    crosses = jnp.logical_and(bend(z) == core, lax.rem(row // half + y + z + 1, 2) != upper)
    gate = jnp.where(upper == 0, depth, depth - 1)
    at_gate = z == jnp.where(upper == 0, depth - 1, depth)
    has_up = jnp.logical_and(z + 1 < planes, (z + 1) // depth == upper)
    has_down = jnp.logical_and(z > 0, (z + planes - 1) // depth - 2 == upper)

    def ways(i):
        source = plane_of(i, 0)
        within = source // depth == upper
        rises = jnp.where(within, z >= source, upper == 1)
        falls = jnp.where(within, z <= source, upper == 0)
        return jnp.logical_and(has_up, rises), jnp.logical_and(has_down, falls)

    home = col // per_row
    slot = z // rows

    barrier = pltpu.get_barrier_semaphore()

    def greet(where):
        pl.semaphore_signal(barrier, inc=1, device_id=where, device_id_type=MESH)

    local_sigma = pltpu.make_async_copy(sigma_ref, own, load.at[0])
    local_u = pltpu.make_async_copy(u_ref.at[0], uown, load.at[1])
    local_inv = pltpu.make_async_copy(inv_ref.at[0], iown, load.at[2])
    expected = jnp.int32(rows)
    number = lambda flag: flag.astype(jnp.int32)
    greet(dev(side))
    for o in range(1, rows):
        greet(dev(col, lax.rem(row + o, rows)))
    pl.when(has_up)(lambda: greet(dev(col + 2)))
    pl.when(has_down)(lambda: greet(dev(col - 2)))
    for i in range(groups):
        other = jnp.logical_and(at_gate, plane_of(i, 0) // depth != upper)
        pl.when(other)(lambda: greet(dev(node_col(i, 0))))
    expected += number(has_up) + number(has_down) + number(crosses)
    local_u.start()
    local_sigma.start()
    local_inv.start()
    pl.semaphore_wait(barrier, expected)

    def a_copy(i, n, way, source):
        return pltpu.make_async_remote_copy(
            source,
            ubuf.at[0, i, n],
            a_send.at[way, i, n],
            a_recv.at[i, n],
            dev(col + 2 - 4 * way),
            MESH,
        )

    def o_copy(n):
        return pltpu.make_async_remote_copy(
            u_ref.at[0, n], ubuf.at[0, slot, n], o_send.at[n], a_recv.at[slot, n], dev(gate * 2 + y), MESH
        )

    def b_copy(i, n, source):
        return pltpu.make_async_remote_copy(
            source, ubuf.at[1, i, n], b_send.at[i, n], b_recv.at[i, n], dev(side), MESH
        )

    def arrival(e, i, n, sems):
        mine = ubuf.at[e, i, n]
        return pltpu.make_async_remote_copy(mine, mine, b_send.at[i, n], sems.at[i, n], dev(side), MESH)

    def pass_on(i, n, source):
        for way, flag in enumerate(ways(i)):
            pl.when(flag)(a_copy(i, n, way, source).start)
        b_copy(i, n, source).start()

    def n_copies(i, source):
        def to(lane, e, where):
            return pltpu.make_async_remote_copy(
                source, sbuf.at[pl.ds(e * groups + i, 1)], n_send.at[lane, i], n_recv.at[e, i], dev(where), MESH
            )

        rises, falls = ways(i)
        return (rises, to(0, 0, col + 2)), (falls, to(1, 0, col - 2)), (True, to(2, 1, side))

    def n_cross():
        return pltpu.make_async_remote_copy(
            s_ref, sbuf.at[pl.ds(slot, 1)], n_send.at[3, 0], n_recv.at[0, slot], dev(gate * 2 + y), MESH
        )

    def n_arrival(e, i):
        mine = sbuf.at[pl.ds(e * groups + i, 1)]
        return pltpu.make_async_remote_copy(mine, mine, n_send.at[2, i], n_recv.at[e, i], dev(side), MESH)

    def x_copy(o, c):
        return pltpu.make_async_remote_copy(
            sigma_ref.at[lax.rem(c, row_count), c // row_count],
            raw.at[row, c],
            x_send.at[o, c],
            s_recv.at[row, c],
            dev(col, lax.rem(row + 2 * o, rows)),
            MESH,
        )

    def own_copy(c):
        return pltpu.make_async_remote_copy(
            sigma_ref.at[lax.rem(c, row_count), c // row_count],
            raw.at[row, c],
            c_send.at[0, c],
            s_recv.at[row, c],
            dev(col, mate),
            MESH,
        )

    def c_copy(o, c):
        r = lax.rem(row + 2 * o, rows)
        return pltpu.make_async_remote_copy(
            raw.at[r, c], raw.at[r, c], c_send.at[o, c], s_recv.at[r, c], dev(col, mate), MESH
        )

    def s_arrival(r, c):
        return pltpu.make_async_remote_copy(
            raw.at[r, c], raw.at[r, c], c_send.at[0, c], s_recv.at[r, c], dev(col, mate), MESH
        )

    blocks = row_count * col_count

    def start_u():
        @pl.when(crosses)
        def _():
            n_cross().start()

            @pl.loop(0, entries)
            def _(n):
                o_copy(n).start()

        for i in range(groups):

            @pl.when(plane_of(i, 0) == z)
            def _():
                for flag, copy in n_copies(i, s_ref):
                    pl.when(flag)(copy.start)

                @pl.loop(0, entries)
                def _(n):
                    pass_on(i, n, u_ref.at[0, n])

    start_u()

    @pl.loop(0, blocks)
    def _(c):
        for o in range(1, half):
            x_copy(o, c).start()

    @pl.loop(0, blocks)
    def _(c):
        own_copy(c).start()

    def member(b):
        found, where = jnp.int32(0), jnp.int32(0)
        for k in range(entries):
            hit = s_ref[0, k] == b
            found, where = jnp.where(hit, 1, found), jnp.where(hit, k, where)
        return found.astype(jnp.float32), where

    def keep(r, c, source):
        high, low = split(source[...].T)
        st_hi[c // row_count, r * row_count + lax.rem(c, row_count)] = high
        st_lo[c // row_count, r * row_count + lax.rem(c, row_count)] = low

    local_u.wait()
    row_start = row * row_count
    found = []
    for a in range(row_count):
        here, where = member(row_start + a)
        found.append(here)
        high, low = split((uown[where] * here).T)
        lanes = slice(a % col_count * width, (a % col_count + 1) * width)
        wt_hi[a // col_count, :, lanes] = high
        wt_lo[a // col_count, :, lanes] = low

    for i in range(groups):

        @pl.when(plane_of(i, 0) == z)
        def _():
            ubuf[0, i] = uown[...]
            for k in range(entries):
                sbuf[i, k] = s_ref[0, k]

    local_sigma.wait()

    @pl.loop(0, blocks)
    def _(c):
        keep(row, c, own.at[lax.rem(c, row_count), c // row_count])

    local_inv.wait()
    inv = iown[...]
    diag_ref[0] = dot_t(inv, inv)

    def s_mated(c):
        for o in range(1, half):
            r = lax.rem(mate + 2 * o, rows)
            s_arrival(r, c).wait_recv()
            keep(r, c, raw.at[r, c])

    def s_forward(c):
        for o in range(1, half):
            r = lax.rem(row + 2 * o, rows)
            s_arrival(r, c).wait_recv()
            c_copy(o, c).start()
            keep(r, c, raw.at[r, c])
        s_arrival(mate, c).wait_recv()
        keep(mate, c, raw.at[mate, c])
        pl.when(c > 0)(lambda: s_mated(c - 1))

    def self_out(i, e):
        return jnp.logical_and(node_col(i, e) == col, home == row)

    def y_copy(i, e, q):
        return pltpu.make_async_remote_copy(
            yout.at[e, i, q],
            yin.at[lax.rem(col, per_row) * col_count + q],
            y_send.at[e, i, q],
            y_recv.at[lax.rem(col, per_row), q],
            dev(node_col(i, e), home),
            MESH,
        )

    def finish(e, i, q):
        def term(k, total):
            picks = [k * pack + p for p in range(pack)]
            high, low = split(jnp.concatenate([ubuf[e, i, p] for p in picks], axis=0))
            near = [sbuf[e * groups + i, p] for p in picks]
            st_h = jnp.concatenate([st_hi[q, b] for b in near], axis=1)
            st_l = jnp.concatenate([st_lo[q, b] for b in near], axis=1)
            both = dot(st_h, jnp.concatenate([high, low], axis=1))
            return total + (both[:, :width] + (both[:, width:] + dot(st_l, high)))

        yout[e, i, q] = lax.fori_loop(
            0,
            entries // pack,
            term,
            jnp.zeros((width, width), jnp.float32),
            unroll=min(entries // pack, 4),
        )

        @pl.when(jnp.logical_not(self_out(i, e)))
        def _():
            y_copy(i, e, q).start()

        @pl.when(self_out(i, e))
        def _():
            yin[lax.rem(col, per_row) * col_count + q] = yout[e, i, q]

    def pace(n):
        return 2 * n * blocks // (3 * entries) + 1

    def late(i):
        first = jnp.where(upper == 0, depth - 1, depth)
        return jnp.where(plane_of(i, 0) // depth == upper, 0, LAG * jnp.abs(z - first))

    steps = entries + LAG * (depth - 1)
    ready = [
        next(t for t in range(3 * entries) if pace(t) >= min((q + 1) * row_count + 1, blocks))
        for q in range(col_count)
    ]
    steps = max(steps, ready[-1] + 1)

    @pl.loop(0, steps)
    def _(t):
        for i in range(groups):
            n = t - late(i)

            @pl.when(jnp.logical_and(plane_of(i, 0) != z, jnp.logical_and(n >= 0, n < entries)))
            def _():
                @pl.when(n == 0)
                def _():
                    n_arrival(0, i).wait_recv()
                    for flag, copy in n_copies(i, sbuf.at[pl.ds(i, 1)]):
                        pl.when(flag)(copy.start)

                arrival(0, i, n, a_recv).wait_recv()
                pass_on(i, n, ubuf.at[0, i, n])

        before = jnp.where(t == 0, 0, pace(t - 1))
        fresh = jnp.logical_and(pace(t) > before, before < blocks)
        pl.when(fresh)(lambda: s_forward(before))
        for i in range(groups):
            for q in range(col_count - 1):
                when = jnp.maximum(ready[q], late(i) + entries - 1)
                pl.when(t == when)(functools.partial(finish, 0, i, q))

    def y_from(i):
        return row * per_row + i

    def y_arrival(i, q):
        mine = yin.at[i * col_count + q]
        return pltpu.make_async_remote_copy(
            mine, mine, y_send.at[0, 0, q], y_recv.at[i, q], dev(side), MESH
        )

    s_mated(blocks - 1)
    for i in range(groups):
        finish(0, i, col_count - 1)
    for i in range(groups):
        n_arrival(1, i).wait_recv()
        for n in range(entries):
            arrival(1, i, n, b_recv).wait_recv()
        for q in range(col_count):
            finish(1, i, q)

    total = jnp.zeros((width, width), jnp.float32)
    for i in range(per_row):
        other = y_from(i)

        @pl.when(jnp.logical_or(other != col, worker(other // 2) != row))
        def _():
            for q in range(col_count):
                y_arrival(i, q).wait_recv()

        panels = []
        for q in range(col_count):
            a = i * col_count + q
            panels.append(-yin[a] * found[a])
            panel_ref[0, a] = panels[q]
        high, low = split(jnp.concatenate(panels, axis=0))
        both = dot(wt_hi[i], jnp.concatenate([high, low], axis=1))
        total += both[:, :width] + (both[:, width:] + dot(wt_lo[i], high))
    share[...] = total

    def d_copy(o):
        return pltpu.make_async_remote_copy(
            share, shares.at[row], d_send.at[o], d_recv.at[row], dev(col, lax.rem(row + o, rows)), MESH
        )

    def d_arrival(r):
        mine = shares.at[r]
        return pltpu.make_async_remote_copy(mine, mine, d_send.at[0], d_recv.at[r], dev(side), MESH)

    for o in range(1, rows):
        d_copy(o).start()

    @pl.loop(0, blocks)
    def _(c):
        own_copy(c).wait_send()
        for o in range(1, half):
            x_copy(o, c).wait_send()
            c_copy(o, c).wait_send()

    @pl.when(crosses)
    def _():
        n_cross().wait_send()

        @pl.loop(0, entries)
        def _(n):
            o_copy(n).wait_send()

    for i in range(groups):
        for flag, copy in n_copies(i, s_ref):
            pl.when(flag)(copy.wait_send)
        for e in range(2):
            for q in range(col_count):
                pl.when(jnp.logical_not(self_out(i, e)))(y_copy(i, e, q).wait_send)

        @pl.loop(0, entries)
        def _(n):
            for way, flag in enumerate(ways(i)):
                pl.when(flag)(a_copy(i, n, way, u_ref.at[0, n]).wait_send)
            b_copy(i, n, u_ref.at[0, n]).wait_send()

    shares[row] = total
    total = -diag_ref[0]
    for r in range(rows):
        pl.when(row != r)(d_arrival(r).wait_recv)
        total += shares[r]
    diag_ref[0] = -total
    for o in range(1, rows):
        d_copy(o).wait_send()


def local(sigma_anc, panel_u, structure, diag_inv):
    row_count, col_count, width = sigma_anc.shape[0], sigma_anc.shape[1], sigma_anc.shape[2]
    entries = panel_u.shape[1]
    cols, rows = lax.axis_size("col"), lax.axis_size("row")
    planes, half = cols // 2, rows // 2
    groups = planes // rows
    per_row = row_count // col_count
    ancestors = rows * row_count
    block = (width, width)
    f32, bf16 = jnp.float32, jnp.bfloat16
    vmem, hbm = pl.BlockSpec(memory_space=pltpu.VMEM), pl.BlockSpec(memory_space=pl.ANY)
    dma = pltpu.SemaphoreType.DMA
    return pl.pallas_call(
        functools.partial(kernel, planes, rows),
        out_shape=(
            jax.ShapeDtypeStruct((1, row_count, *block), f32),
            jax.ShapeDtypeStruct((1, *block), f32),
        ),
        in_specs=[hbm, hbm, pl.BlockSpec(memory_space=pltpu.SMEM), hbm],
        out_specs=(vmem, vmem),
        scratch_shapes=[
            pltpu.VMEM((row_count, col_count, *block), f32),
            pltpu.VMEM((rows, row_count * col_count, *block), f32),
            pltpu.VMEM((col_count, ancestors, *block), bf16),
            pltpu.VMEM((col_count, ancestors, *block), bf16),
            pltpu.VMEM((entries, *block), f32),
            pltpu.VMEM(block, f32),
            pltpu.VMEM((2, groups, entries, *block), f32),
            pltpu.SMEM((2 * groups, entries), jnp.int32),
            pltpu.VMEM((per_row, width, col_count * width), bf16),
            pltpu.VMEM((per_row, width, col_count * width), bf16),
            pltpu.VMEM((2, groups, col_count, *block), f32),
            pltpu.VMEM((row_count, *block), f32),
            pltpu.VMEM(block, f32),
            pltpu.VMEM((rows, *block), f32),
            dma((half, row_count * col_count)),
            dma((half, row_count * col_count)),
            dma((rows, row_count * col_count)),
            dma((2, groups, entries)),
            dma((entries,)),
            dma((groups, entries)),
            dma((groups, entries)),
            dma((groups, entries)),
            dma((4, groups)),
            dma((2, groups)),
            dma((2, groups, col_count)),
            dma((per_row, col_count)),
            dma((rows,)),
            dma((rows,)),
            dma((3,)),
        ],
        compiler_params=pltpu.CompilerParams(
            collective_id=0, has_side_effects=True, vmem_limit_bytes=48 * 1024 * 1024
        ),
    )(*(pltpu.with_memory_space_constraint(v, pltpu.HBM) for v in (sigma_anc, panel_u, structure, diag_inv)))


def solution(mesh):
    placed = (
        P("row", "col", None, None),
        P("col", None, None, None),
        P("col", None),
        P("col", None, None),
    )
    return jax.shard_map(
        local,
        mesh=mesh,
        in_specs=placed,
        out_specs=(P("col", "row", None, None), P("col", None, None)),
        check_vma=False,
    )
```

```python
import functools

import jax
import jax.numpy as jnp
from jax import lax
from jax.experimental import pallas as pl
from jax.experimental.pallas import tpu as pltpu
from jax.sharding import PartitionSpec as P

MESH = pl.DeviceIdType.MESH
HIGHEST = lax.Precision.HIGHEST
LAG = 3


def split(x):
    high = x.astype(jnp.bfloat16)
    return high, (x - high.astype(jnp.float32)).astype(jnp.bfloat16)


def dot(a, b):
    return jnp.dot(a, b, preferred_element_type=jnp.float32)


def dot_t(a, b):
    return lax.dot_general(
        a, b, (((0,), (0,)), ((), ())), precision=HIGHEST, preferred_element_type=jnp.float32
    )


def bend(plane):
    return lax.rem((plane + 1) // 2, 2)


def kernel(
    planes,
    rows,
    sigma_ref,
    u_ref,
    s_ref,
    inv_ref,
    panel_ref,
    diag_ref,
    own,
    raw,
    st_hi,
    st_lo,
    uown,
    iown,
    ubuf,
    sbuf,
    wt_hi,
    wt_lo,
    yout,
    yin,
    share,
    shares,
    x_send,
    c_send,
    s_recv,
    a_send,
    o_send,
    a_recv,
    b_send,
    b_recv,
    n_send,
    n_recv,
    y_send,
    y_recv,
    d_send,
    d_recv,
    load,
):
    row_count, col_count, width = sigma_ref.shape[0], sigma_ref.shape[1], sigma_ref.shape[2]
    entries, groups = u_ref.shape[1], planes // rows
    half = rows // 2
    pack = 2 - entries % 2
    per_row = row_count // col_count
    col, row = lax.axis_index("col"), lax.axis_index("row")
    z, y = col // 2, lax.rem(col, 2)
    core = lax.rem(row, 2)
    mate, side = row + 1 - 2 * core, col + 1 - 2 * y

    def dev(c, r=None):
        return {"col": c, "row": row if r is None else r}

    depth = planes // 2
    upper = z // depth
    even = lax.rem(row // half + upper + y + 1, 2)

    def plane_of(i, e):
        odd = jnp.where(e == 0, even, 1 - even)
        return rows * i + jnp.where(core == 0, 3 * odd, 2 - odd)

    def node_col(i, e):
        return plane_of(i, e) * 2 + jnp.where(e == 0, y, 1 - y)

    def worker(other):
        return half * lax.rem(y + z + other // depth + 1, 2) + bend(z)

    crosses = jnp.logical_and(bend(z) == core, lax.rem(row // half + y + z + 1, 2) != upper)
    gate = jnp.where(upper == 0, depth, depth - 1)
    at_gate = z == jnp.where(upper == 0, depth - 1, depth)
    has_up = jnp.logical_and(z + 1 < planes, (z + 1) // depth == upper)
    has_down = jnp.logical_and(z > 0, (z + planes - 1) // depth - 2 == upper)

    def ways(i):
        source = plane_of(i, 0)
        within = source // depth == upper
        rises = jnp.where(within, z >= source, upper == 1)
        falls = jnp.where(within, z <= source, upper == 0)
        return jnp.logical_and(has_up, rises), jnp.logical_and(has_down, falls)

    home = col // per_row
    slot = z // rows

    barrier = pltpu.get_barrier_semaphore()

    def greet(where):
        pl.semaphore_signal(barrier, inc=1, device_id=where, device_id_type=MESH)

    local_sigma = pltpu.make_async_copy(sigma_ref, own, load.at[0])
    local_u = pltpu.make_async_copy(u_ref.at[0], uown, load.at[1])
    local_inv = pltpu.make_async_copy(inv_ref.at[0], iown, load.at[2])
    expected = jnp.int32(rows)
    number = lambda flag: flag.astype(jnp.int32)
    greet(dev(side))
    for o in range(1, rows):
        greet(dev(col, lax.rem(row + o, rows)))
    pl.when(has_up)(lambda: greet(dev(col + 2)))
    pl.when(has_down)(lambda: greet(dev(col - 2)))
    for i in range(groups):
        other = jnp.logical_and(at_gate, plane_of(i, 0) // depth != upper)
        pl.when(other)(lambda: greet(dev(node_col(i, 0))))
    expected += number(has_up) + number(has_down) + number(crosses)
    local_u.start()
    local_sigma.start()
    local_inv.start()
    pl.semaphore_wait(barrier, expected)

    def a_copy(i, n, way, source):
        return pltpu.make_async_remote_copy(
            source,
            ubuf.at[0, i, n],
            a_send.at[way, i, n],
            a_recv.at[i, n],
            dev(col + 2 - 4 * way),
            MESH,
        )

    def o_copy(n):
        return pltpu.make_async_remote_copy(
            u_ref.at[0, n], ubuf.at[0, slot, n], o_send.at[n], a_recv.at[slot, n], dev(gate * 2 + y), MESH
        )

    def b_copy(i, n, source):
        return pltpu.make_async_remote_copy(
            source, ubuf.at[1, i, n], b_send.at[i, n], b_recv.at[i, n], dev(side), MESH
        )

    def arrival(e, i, n, sems):
        mine = ubuf.at[e, i, n]
        return pltpu.make_async_remote_copy(mine, mine, b_send.at[i, n], sems.at[i, n], dev(side), MESH)

    def pass_on(i, n, source):
        for way, flag in enumerate(ways(i)):
            pl.when(flag)(a_copy(i, n, way, source).start)
        b_copy(i, n, source).start()

    def n_copies(i, source):
        def to(lane, e, where):
            return pltpu.make_async_remote_copy(
                source, sbuf.at[pl.ds(e * groups + i, 1)], n_send.at[lane, i], n_recv.at[e, i], dev(where), MESH
            )

        rises, falls = ways(i)
        return (rises, to(0, 0, col + 2)), (falls, to(1, 0, col - 2)), (True, to(2, 1, side))

    def n_cross():
        return pltpu.make_async_remote_copy(
            s_ref, sbuf.at[pl.ds(slot, 1)], n_send.at[3, 0], n_recv.at[0, slot], dev(gate * 2 + y), MESH
        )

    def n_arrival(e, i):
        mine = sbuf.at[pl.ds(e * groups + i, 1)]
        return pltpu.make_async_remote_copy(mine, mine, n_send.at[2, i], n_recv.at[e, i], dev(side), MESH)

    def x_copy(o, c):
        return pltpu.make_async_remote_copy(
            sigma_ref.at[lax.rem(c, row_count), c // row_count],
            raw.at[row, c],
            x_send.at[o, c],
            s_recv.at[row, c],
            dev(col, lax.rem(row + 2 * o, rows)),
            MESH,
        )

    def own_copy(c):
        return pltpu.make_async_remote_copy(
            sigma_ref.at[lax.rem(c, row_count), c // row_count],
            raw.at[row, c],
            c_send.at[0, c],
            s_recv.at[row, c],
            dev(col, mate),
            MESH,
        )

    def c_copy(o, c):
        r = lax.rem(row + 2 * o, rows)
        return pltpu.make_async_remote_copy(
            raw.at[r, c], raw.at[r, c], c_send.at[o, c], s_recv.at[r, c], dev(col, mate), MESH
        )

    def s_arrival(r, c):
        return pltpu.make_async_remote_copy(
            raw.at[r, c], raw.at[r, c], c_send.at[0, c], s_recv.at[r, c], dev(col, mate), MESH
        )

    blocks = row_count * col_count

    def start_u():
        @pl.when(crosses)
        def _():
            n_cross().start()

            @pl.loop(0, entries)
            def _(n):
                o_copy(n).start()

        for i in range(groups):

            @pl.when(plane_of(i, 0) == z)
            def _():
                for flag, copy in n_copies(i, s_ref):
                    pl.when(flag)(copy.start)

                @pl.loop(0, entries)
                def _(n):
                    pass_on(i, n, u_ref.at[0, n])

    start_u()

    @pl.loop(0, blocks)
    def _(c):
        for o in range(1, half):
            x_copy(o, c).start()

    @pl.loop(0, blocks)
    def _(c):
        own_copy(c).start()

    def member(b):
        found, where = jnp.int32(0), jnp.int32(0)
        for k in range(entries):
            hit = s_ref[0, k] == b
            found, where = jnp.where(hit, 1, found), jnp.where(hit, k, where)
        return found.astype(jnp.float32), where

    def keep(r, c, source):
        high, low = split(source[...].T)
        st_hi[c // row_count, r * row_count + lax.rem(c, row_count)] = high
        st_lo[c // row_count, r * row_count + lax.rem(c, row_count)] = low

    local_u.wait()
    row_start = row * row_count
    found = []
    for a in range(row_count):
        here, where = member(row_start + a)
        found.append(here)
        high, low = split((uown[where] * here).T)
        lanes = slice(a % col_count * width, (a % col_count + 1) * width)
        wt_hi[a // col_count, :, lanes] = high
        wt_lo[a // col_count, :, lanes] = low

    for i in range(groups):

        @pl.when(plane_of(i, 0) == z)
        def _():
            ubuf[0, i] = uown[...]
            for k in range(entries):
                sbuf[i, k] = s_ref[0, k]

    local_sigma.wait()

    @pl.loop(0, blocks)
    def _(c):
        keep(row, c, own.at[lax.rem(c, row_count), c // row_count])

    local_inv.wait()
    inv = iown[...]
    diag_ref[0] = dot_t(inv, inv)

    def s_mated(c):
        for o in range(1, half):
            r = lax.rem(mate + 2 * o, rows)
            s_arrival(r, c).wait_recv()
            keep(r, c, raw.at[r, c])

    def s_forward(c):
        for o in range(1, half):
            r = lax.rem(row + 2 * o, rows)
            s_arrival(r, c).wait_recv()
            c_copy(o, c).start()
            keep(r, c, raw.at[r, c])
        s_arrival(mate, c).wait_recv()
        keep(mate, c, raw.at[mate, c])
        pl.when(c > 0)(lambda: s_mated(c - 1))

    def self_out(i, e):
        return jnp.logical_and(node_col(i, e) == col, home == row)

    def y_copy(i, e, q):
        return pltpu.make_async_remote_copy(
            yout.at[e, i, q],
            yin.at[lax.rem(col, per_row) * col_count + q],
            y_send.at[e, i, q],
            y_recv.at[lax.rem(col, per_row), q],
            dev(node_col(i, e), home),
            MESH,
        )

    def finish(e, i, q):
        def term(k, total):
            picks = [k * pack + p for p in range(pack)]
            high, low = split(jnp.concatenate([ubuf[e, i, p] for p in picks], axis=0))
            near = [sbuf[e * groups + i, p] for p in picks]
            st_h = jnp.concatenate([st_hi[q, b] for b in near], axis=1)
            st_l = jnp.concatenate([st_lo[q, b] for b in near], axis=1)
            both = dot(st_h, jnp.concatenate([high, low], axis=1))
            return total + (both[:, :width] + (both[:, width:] + dot(st_l, high)))

        yout[e, i, q] = lax.fori_loop(
            0,
            entries // pack,
            term,
            jnp.zeros((width, width), jnp.float32),
            unroll=min(entries // pack, 4),
        )

        @pl.when(jnp.logical_not(self_out(i, e)))
        def _():
            y_copy(i, e, q).start()

        @pl.when(self_out(i, e))
        def _():
            yin[lax.rem(col, per_row) * col_count + q] = yout[e, i, q]

    def pace(n):
        return n * blocks // (2 * entries) + 1

    def late(i):
        first = jnp.where(upper == 0, depth - 1, depth)
        return jnp.where(plane_of(i, 0) // depth == upper, 0, LAG * jnp.abs(z - first))

    steps = entries + LAG * (depth - 1)
    ready = [
        next(t for t in range(3 * entries) if pace(t) >= min((q + 1) * row_count + 1, blocks))
        for q in range(col_count)
    ]
    steps = max(steps, ready[-1] + 1)

    @pl.loop(0, steps)
    def _(t):
        for i in range(groups):
            n = t - late(i)

            @pl.when(jnp.logical_and(plane_of(i, 0) != z, jnp.logical_and(n >= 0, n < entries)))
            def _():
                @pl.when(n == 0)
                def _():
                    n_arrival(0, i).wait_recv()
                    for flag, copy in n_copies(i, sbuf.at[pl.ds(i, 1)]):
                        pl.when(flag)(copy.start)

                arrival(0, i, n, a_recv).wait_recv()
                pass_on(i, n, ubuf.at[0, i, n])

        before = jnp.where(t == 0, 0, pace(t - 1))
        fresh = jnp.logical_and(pace(t) > before, before < blocks)
        pl.when(fresh)(lambda: s_forward(before))
        for i in range(groups):
            for q in range(col_count - 1):
                when = jnp.maximum(ready[q], late(i) + entries - 1)
                pl.when(t == when)(functools.partial(finish, 0, i, q))

    def y_from(i):
        return row * per_row + i

    def y_arrival(i, q):
        mine = yin.at[i * col_count + q]
        return pltpu.make_async_remote_copy(
            mine, mine, y_send.at[0, 0, q], y_recv.at[i, q], dev(side), MESH
        )

    s_mated(blocks - 1)
    for i in range(groups):
        finish(0, i, col_count - 1)
    for i in range(groups):
        n_arrival(1, i).wait_recv()
        for n in range(entries):
            arrival(1, i, n, b_recv).wait_recv()
        for q in range(col_count):
            finish(1, i, q)

    total = jnp.zeros((width, width), jnp.float32)
    for i in range(per_row):
        other = y_from(i)

        @pl.when(jnp.logical_or(other != col, worker(other // 2) != row))
        def _():
            for q in range(col_count):
                y_arrival(i, q).wait_recv()

        panels = []
        for q in range(col_count):
            a = i * col_count + q
            panels.append(-yin[a] * found[a])
            panel_ref[0, a] = panels[q]
        high, low = split(jnp.concatenate(panels, axis=0))
        both = dot(wt_hi[i], jnp.concatenate([high, low], axis=1))
        total += both[:, :width] + (both[:, width:] + dot(wt_lo[i], high))
    share[...] = total

    def d_copy(o):
        return pltpu.make_async_remote_copy(
            share, shares.at[row], d_send.at[o], d_recv.at[row], dev(col, lax.rem(row + o, rows)), MESH
        )

    def d_arrival(r):
        mine = shares.at[r]
        return pltpu.make_async_remote_copy(mine, mine, d_send.at[0], d_recv.at[r], dev(side), MESH)

    for o in range(1, rows):
        d_copy(o).start()

    @pl.loop(0, blocks)
    def _(c):
        own_copy(c).wait_send()
        for o in range(1, half):
            x_copy(o, c).wait_send()
            c_copy(o, c).wait_send()

    @pl.when(crosses)
    def _():
        n_cross().wait_send()

        @pl.loop(0, entries)
        def _(n):
            o_copy(n).wait_send()

    for i in range(groups):
        for flag, copy in n_copies(i, s_ref):
            pl.when(flag)(copy.wait_send)
        for e in range(2):
            for q in range(col_count):
                pl.when(jnp.logical_not(self_out(i, e)))(y_copy(i, e, q).wait_send)

        @pl.loop(0, entries)
        def _(n):
            for way, flag in enumerate(ways(i)):
                pl.when(flag)(a_copy(i, n, way, u_ref.at[0, n]).wait_send)
            b_copy(i, n, u_ref.at[0, n]).wait_send()

    shares[row] = total
    total = -diag_ref[0]
    for r in range(rows):
        pl.when(row != r)(d_arrival(r).wait_recv)
        total += shares[r]
    diag_ref[0] = -total
    for o in range(1, rows):
        d_copy(o).wait_send()


def local(sigma_anc, panel_u, structure, diag_inv):
    row_count, col_count, width = sigma_anc.shape[0], sigma_anc.shape[1], sigma_anc.shape[2]
    entries = panel_u.shape[1]
    cols, rows = lax.axis_size("col"), lax.axis_size("row")
    planes, half = cols // 2, rows // 2
    groups = planes // rows
    per_row = row_count // col_count
    ancestors = rows * row_count
    block = (width, width)
    f32, bf16 = jnp.float32, jnp.bfloat16
    vmem, hbm = pl.BlockSpec(memory_space=pltpu.VMEM), pl.BlockSpec(memory_space=pl.ANY)
    dma = pltpu.SemaphoreType.DMA
    return pl.pallas_call(
        functools.partial(kernel, planes, rows),
        out_shape=(
            jax.ShapeDtypeStruct((1, row_count, *block), f32),
            jax.ShapeDtypeStruct((1, *block), f32),
        ),
        in_specs=[hbm, hbm, pl.BlockSpec(memory_space=pltpu.SMEM), hbm],
        out_specs=(vmem, vmem),
        scratch_shapes=[
            pltpu.VMEM((row_count, col_count, *block), f32),
            pltpu.VMEM((rows, row_count * col_count, *block), f32),
            pltpu.VMEM((col_count, ancestors, *block), bf16),
            pltpu.VMEM((col_count, ancestors, *block), bf16),
            pltpu.VMEM((entries, *block), f32),
            pltpu.VMEM(block, f32),
            pltpu.VMEM((2, groups, entries, *block), f32),
            pltpu.SMEM((2 * groups, entries), jnp.int32),
            pltpu.VMEM((per_row, width, col_count * width), bf16),
            pltpu.VMEM((per_row, width, col_count * width), bf16),
            pltpu.VMEM((2, groups, col_count, *block), f32),
            pltpu.VMEM((row_count, *block), f32),
            pltpu.VMEM(block, f32),
            pltpu.VMEM((rows, *block), f32),
            dma((half, row_count * col_count)),
            dma((half, row_count * col_count)),
            dma((rows, row_count * col_count)),
            dma((2, groups, entries)),
            dma((entries,)),
            dma((groups, entries)),
            dma((groups, entries)),
            dma((groups, entries)),
            dma((4, groups)),
            dma((2, groups)),
            dma((2, groups, col_count)),
            dma((per_row, col_count)),
            dma((rows,)),
            dma((rows,)),
            dma((3,)),
        ],
        compiler_params=pltpu.CompilerParams(
            collective_id=0, has_side_effects=True, vmem_limit_bytes=48 * 1024 * 1024
        ),
    )(*(pltpu.with_memory_space_constraint(v, pltpu.HBM) for v in (sigma_anc, panel_u, structure, diag_inv)))


def solution(mesh):
    placed = (
        P("row", "col", None, None),
        P("col", None, None, None),
        P("col", None),
        P("col", None, None),
    )
    return jax.shard_map(
        local,
        mesh=mesh,
        in_specs=placed,
        out_specs=(P("col", "row", None, None), P("col", None, None)),
        check_vma=False,
    )
```

```python
import functools

import jax
import jax.numpy as jnp
from jax import lax
from jax.experimental import pallas as pl
from jax.experimental.pallas import tpu as pltpu
from jax.sharding import PartitionSpec as P

MESH = pl.DeviceIdType.MESH
HIGHEST = lax.Precision.HIGHEST
LAG = 3


def split(x):
    high = x.astype(jnp.bfloat16)
    return high, (x - high.astype(jnp.float32)).astype(jnp.bfloat16)


def dot(a, b):
    return jnp.dot(a, b, preferred_element_type=jnp.float32)


def dot_t(a, b):
    return lax.dot_general(
        a, b, (((0,), (0,)), ((), ())), precision=HIGHEST, preferred_element_type=jnp.float32
    )


def bend(plane):
    return lax.rem((plane + 1) // 2, 2)


def kernel(
    planes,
    rows,
    sigma_ref,
    u_ref,
    s_hbm,
    inv_ref,
    panel_ref,
    diag_ref,
    s_ref,
    own,
    raw,
    st_hi,
    st_lo,
    uown,
    iown,
    ubuf,
    sbuf,
    wt_hi,
    wt_lo,
    yout,
    yin,
    share,
    shares,
    x_send,
    c_send,
    s_recv,
    a_send,
    o_send,
    a_recv,
    b_send,
    b_recv,
    n_send,
    n_recv,
    y_send,
    y_recv,
    d_send,
    d_recv,
    load,
):
    row_count, col_count, width = sigma_ref.shape[0], sigma_ref.shape[1], sigma_ref.shape[2]
    entries, groups = u_ref.shape[1], planes // rows
    half = rows // 2
    pack = 2 - entries % 2
    per_row = row_count // col_count
    col, row = lax.axis_index("col"), lax.axis_index("row")
    z, y = col // 2, lax.rem(col, 2)
    core = lax.rem(row, 2)
    mate, side = row + 1 - 2 * core, col + 1 - 2 * y

    def dev(c, r=None):
        return {"col": c, "row": row if r is None else r}

    depth = planes // 2
    upper = z // depth
    even = lax.rem(row // half + upper + y + 1, 2)

    def plane_of(i, e):
        odd = jnp.where(e == 0, even, 1 - even)
        return rows * i + jnp.where(core == 0, 3 * odd, 2 - odd)

    def node_col(i, e):
        return plane_of(i, e) * 2 + jnp.where(e == 0, y, 1 - y)

    def worker(other):
        return half * lax.rem(y + z + other // depth + 1, 2) + bend(z)

    crosses = jnp.logical_and(bend(z) == core, lax.rem(row // half + y + z + 1, 2) != upper)
    gate = jnp.where(upper == 0, depth, depth - 1)
    at_gate = z == jnp.where(upper == 0, depth - 1, depth)
    has_up = jnp.logical_and(z + 1 < planes, (z + 1) // depth == upper)
    has_down = jnp.logical_and(z > 0, (z + planes - 1) // depth - 2 == upper)

    def ways(i):
        source = plane_of(i, 0)
        within = source // depth == upper
        rises = jnp.where(within, z >= source, upper == 1)
        falls = jnp.where(within, z <= source, upper == 0)
        return jnp.logical_and(has_up, rises), jnp.logical_and(has_down, falls)

    home = col // per_row
    slot = z // rows

    barrier = pltpu.get_barrier_semaphore()

    def greet(where):
        pl.semaphore_signal(barrier, inc=1, device_id=where, device_id_type=MESH)

    local_sigma = pltpu.make_async_copy(sigma_ref, own, load.at[0])
    local_u = pltpu.make_async_copy(u_ref.at[0], uown, load.at[1])
    local_inv = pltpu.make_async_copy(inv_ref.at[0], iown, load.at[2])
    expected = jnp.int32(rows)
    number = lambda flag: flag.astype(jnp.int32)
    greet(dev(side))
    for o in range(1, rows):
        greet(dev(col, lax.rem(row + o, rows)))
    pl.when(has_up)(lambda: greet(dev(col + 2)))
    pl.when(has_down)(lambda: greet(dev(col - 2)))
    for i in range(groups):
        other = jnp.logical_and(at_gate, plane_of(i, 0) // depth != upper)
        pl.when(other)(lambda: greet(dev(node_col(i, 0))))
    expected += number(has_up) + number(has_down) + number(crosses)
    local_s = pltpu.make_async_copy(s_hbm, s_ref, load.at[3])
    local_s.start()
    local_u.start()
    local_sigma.start()
    local_inv.start()
    pl.semaphore_wait(barrier, expected)
    local_s.wait()

    def a_copy(i, n, way, source):
        return pltpu.make_async_remote_copy(
            source,
            ubuf.at[0, i, n],
            a_send.at[way, i, n],
            a_recv.at[i, n],
            dev(col + 2 - 4 * way),
            MESH,
        )

    def o_copy(n):
        return pltpu.make_async_remote_copy(
            u_ref.at[0, n], ubuf.at[0, slot, n], o_send.at[n], a_recv.at[slot, n], dev(gate * 2 + y), MESH
        )

    def b_copy(i, n, source):
        return pltpu.make_async_remote_copy(
            source, ubuf.at[1, i, n], b_send.at[i, n], b_recv.at[i, n], dev(side), MESH
        )

    def arrival(e, i, n, sems):
        mine = ubuf.at[e, i, n]
        return pltpu.make_async_remote_copy(mine, mine, b_send.at[i, n], sems.at[i, n], dev(side), MESH)

    def pass_on(i, n, source):
        for way, flag in enumerate(ways(i)):
            pl.when(flag)(a_copy(i, n, way, source).start)
        b_copy(i, n, source).start()

    def n_copies(i, source):
        def to(lane, e, where):
            return pltpu.make_async_remote_copy(
                source, sbuf.at[pl.ds(e * groups + i, 1)], n_send.at[lane, i], n_recv.at[e, i], dev(where), MESH
            )

        rises, falls = ways(i)
        return (rises, to(0, 0, col + 2)), (falls, to(1, 0, col - 2)), (True, to(2, 1, side))

    def n_cross():
        return pltpu.make_async_remote_copy(
            s_ref, sbuf.at[pl.ds(slot, 1)], n_send.at[3, 0], n_recv.at[0, slot], dev(gate * 2 + y), MESH
        )

    def n_arrival(e, i):
        mine = sbuf.at[pl.ds(e * groups + i, 1)]
        return pltpu.make_async_remote_copy(mine, mine, n_send.at[2, i], n_recv.at[e, i], dev(side), MESH)

    def x_copy(o, c):
        return pltpu.make_async_remote_copy(
            sigma_ref.at[lax.rem(c, row_count), c // row_count],
            raw.at[row, c],
            x_send.at[o, c],
            s_recv.at[row, c],
            dev(col, lax.rem(row + 2 * o, rows)),
            MESH,
        )

    def own_copy(c):
        return pltpu.make_async_remote_copy(
            sigma_ref.at[lax.rem(c, row_count), c // row_count],
            raw.at[row, c],
            c_send.at[0, c],
            s_recv.at[row, c],
            dev(col, mate),
            MESH,
        )

    def c_copy(o, c):
        r = lax.rem(row + 2 * o, rows)
        return pltpu.make_async_remote_copy(
            raw.at[r, c], raw.at[r, c], c_send.at[o, c], s_recv.at[r, c], dev(col, mate), MESH
        )

    def s_arrival(r, c):
        return pltpu.make_async_remote_copy(
            raw.at[r, c], raw.at[r, c], c_send.at[0, c], s_recv.at[r, c], dev(col, mate), MESH
        )

    blocks = row_count * col_count

    def start_u():
        @pl.when(crosses)
        def _():
            n_cross().start()

            @pl.loop(0, entries)
            def _(n):
                o_copy(n).start()

        for i in range(groups):

            @pl.when(plane_of(i, 0) == z)
            def _():
                for flag, copy in n_copies(i, s_ref):
                    pl.when(flag)(copy.start)

                @pl.loop(0, entries)
                def _(n):
                    pass_on(i, n, u_ref.at[0, n])

    start_u()

    @pl.loop(0, blocks)
    def _(c):
        for o in range(1, half):
            x_copy(o, c).start()

    @pl.loop(0, blocks)
    def _(c):
        own_copy(c).start()

    def member(b):
        found, where = jnp.int32(0), jnp.int32(0)
        for k in range(entries):
            hit = s_ref[0, k] == b
            found, where = jnp.where(hit, 1, found), jnp.where(hit, k, where)
        return found.astype(jnp.float32), where

    def keep(r, c, source):
        high, low = split(source[...].T)
        st_hi[c // row_count, r * row_count + lax.rem(c, row_count)] = high
        st_lo[c // row_count, r * row_count + lax.rem(c, row_count)] = low

    local_u.wait()
    for i in range(groups):

        @pl.when(plane_of(i, 0) == z)
        def _():
            ubuf[0, i] = uown[...]
            for k in range(entries):
                sbuf[i, k] = s_ref[0, k]

    local_sigma.wait()

    @pl.loop(0, blocks)
    def _(c):
        keep(row, c, own.at[lax.rem(c, row_count), c // row_count])

    def s_mated(c):
        for o in range(1, half):
            r = lax.rem(mate + 2 * o, rows)
            s_arrival(r, c).wait_recv()
            keep(r, c, raw.at[r, c])

    def s_forward(c):
        for o in range(1, half):
            r = lax.rem(row + 2 * o, rows)
            s_arrival(r, c).wait_recv()
            c_copy(o, c).start()
            keep(r, c, raw.at[r, c])
        s_arrival(mate, c).wait_recv()
        keep(mate, c, raw.at[mate, c])
        pl.when(c > 0)(lambda: s_mated(c - 1))

    def self_out(i, e):
        return jnp.logical_and(node_col(i, e) == col, home == row)

    def y_copy(i, e, q):
        return pltpu.make_async_remote_copy(
            yout.at[e, i, q],
            yin.at[lax.rem(col, per_row) * col_count + q],
            y_send.at[e, i, q],
            y_recv.at[lax.rem(col, per_row), q],
            dev(node_col(i, e), home),
            MESH,
        )

    def finish(e, i, q):
        def term(k, total):
            picks = [k * pack + p for p in range(pack)]
            high, low = split(jnp.concatenate([ubuf[e, i, p] for p in picks], axis=0))
            near = [sbuf[e * groups + i, p] for p in picks]
            st_h = jnp.concatenate([st_hi[q, b] for b in near], axis=1)
            st_l = jnp.concatenate([st_lo[q, b] for b in near], axis=1)
            both = dot(st_h, jnp.concatenate([high, low], axis=1))
            return total + (both[:, :width] + (both[:, width:] + dot(st_l, high)))

        yout[e, i, q] = lax.fori_loop(
            0,
            entries // pack,
            term,
            jnp.zeros((width, width), jnp.float32),
            unroll=min(entries // pack, 4),
        )

        @pl.when(jnp.logical_not(self_out(i, e)))
        def _():
            y_copy(i, e, q).start()

        @pl.when(self_out(i, e))
        def _():
            yin[lax.rem(col, per_row) * col_count + q] = yout[e, i, q]

    def pace(n):
        return n * blocks // (2 * entries) + 1

    def late(i):
        first = jnp.where(upper == 0, depth - 1, depth)
        return jnp.where(plane_of(i, 0) // depth == upper, 0, LAG * jnp.abs(z - first))

    steps = entries + LAG * (depth - 1)
    ready = [
        next(t for t in range(3 * entries) if pace(t) >= min((q + 1) * row_count + 1, blocks))
        for q in range(col_count)
    ]
    steps = max(steps, ready[-1] + 1)

    @pl.loop(0, steps)
    def _(t):
        for i in range(groups):
            n = t - late(i)

            @pl.when(jnp.logical_and(plane_of(i, 0) != z, jnp.logical_and(n >= 0, n < entries)))
            def _():
                @pl.when(n == 0)
                def _():
                    n_arrival(0, i).wait_recv()
                    for flag, copy in n_copies(i, sbuf.at[pl.ds(i, 1)]):
                        pl.when(flag)(copy.start)

                arrival(0, i, n, a_recv).wait_recv()
                pass_on(i, n, ubuf.at[0, i, n])

        before = jnp.where(t == 0, 0, pace(t - 1))
        fresh = jnp.logical_and(pace(t) > before, before < blocks)
        pl.when(fresh)(lambda: s_forward(before))
        for i in range(groups):
            for q in range(col_count - 1):
                when = jnp.maximum(ready[q], late(i) + entries - 1)
                pl.when(t == when)(functools.partial(finish, 0, i, q))

    def y_from(i):
        return row * per_row + i

    def y_arrival(i, q):
        mine = yin.at[i * col_count + q]
        return pltpu.make_async_remote_copy(
            mine, mine, y_send.at[0, 0, q], y_recv.at[i, q], dev(side), MESH
        )

    s_mated(blocks - 1)
    for i in range(groups):
        finish(0, i, col_count - 1)
    for i in range(groups):
        n_arrival(1, i).wait_recv()
        for n in range(entries):
            arrival(1, i, n, b_recv).wait_recv()
        for q in range(col_count):
            finish(1, i, q)

    row_start = row * row_count
    found = []
    for a in range(row_count):
        here, where = member(row_start + a)
        found.append(here)
        high, low = split((uown[where] * here).T)
        lanes = slice(a % col_count * width, (a % col_count + 1) * width)
        wt_hi[a // col_count, :, lanes] = high
        wt_lo[a // col_count, :, lanes] = low

    total = jnp.zeros((width, width), jnp.float32)
    for i in range(per_row):
        other = y_from(i)

        @pl.when(jnp.logical_or(other != col, worker(other // 2) != row))
        def _():
            for q in range(col_count):
                y_arrival(i, q).wait_recv()

        panels = []
        for q in range(col_count):
            a = i * col_count + q
            panels.append(-yin[a] * found[a])
            panel_ref[0, a] = panels[q]
        high, low = split(jnp.concatenate(panels, axis=0))
        both = dot(wt_hi[i], jnp.concatenate([high, low], axis=1))
        total += both[:, :width] + (both[:, width:] + dot(wt_lo[i], high))
    share[...] = total

    def d_copy(o):
        return pltpu.make_async_remote_copy(
            share, shares.at[row], d_send.at[o], d_recv.at[row], dev(col, lax.rem(row + o, rows)), MESH
        )

    def d_arrival(r):
        mine = shares.at[r]
        return pltpu.make_async_remote_copy(mine, mine, d_send.at[0], d_recv.at[r], dev(side), MESH)

    for o in range(1, rows):
        d_copy(o).start()

    local_inv.wait()
    inv = iown[...]
    diag_ref[0] = dot_t(inv, inv)

    @pl.loop(0, blocks)
    def _(c):
        own_copy(c).wait_send()
        for o in range(1, half):
            x_copy(o, c).wait_send()
            c_copy(o, c).wait_send()

    @pl.when(crosses)
    def _():
        n_cross().wait_send()

        @pl.loop(0, entries)
        def _(n):
            o_copy(n).wait_send()

    for i in range(groups):
        for flag, copy in n_copies(i, s_ref):
            pl.when(flag)(copy.wait_send)
        for e in range(2):
            for q in range(col_count):
                pl.when(jnp.logical_not(self_out(i, e)))(y_copy(i, e, q).wait_send)

        @pl.loop(0, entries)
        def _(n):
            for way, flag in enumerate(ways(i)):
                pl.when(flag)(a_copy(i, n, way, u_ref.at[0, n]).wait_send)
            b_copy(i, n, u_ref.at[0, n]).wait_send()

    shares[row] = total
    total = -diag_ref[0]
    for r in range(rows):
        pl.when(row != r)(d_arrival(r).wait_recv)
        total += shares[r]
    diag_ref[0] = -total
    for o in range(1, rows):
        d_copy(o).wait_send()


def local(sigma_anc, panel_u, structure, diag_inv):
    row_count, col_count, width = sigma_anc.shape[0], sigma_anc.shape[1], sigma_anc.shape[2]
    entries = panel_u.shape[1]
    cols, rows = lax.axis_size("col"), lax.axis_size("row")
    planes, half = cols // 2, rows // 2
    groups = planes // rows
    per_row = row_count // col_count
    ancestors = rows * row_count
    block = (width, width)
    f32, bf16 = jnp.float32, jnp.bfloat16
    vmem, hbm = pl.BlockSpec(memory_space=pltpu.VMEM), pl.BlockSpec(memory_space=pl.ANY)
    dma = pltpu.SemaphoreType.DMA
    return pl.pallas_call(
        functools.partial(kernel, planes, rows),
        out_shape=(
            jax.ShapeDtypeStruct((1, row_count, *block), f32),
            jax.ShapeDtypeStruct((1, *block), f32),
        ),
        in_specs=[hbm, hbm, hbm, hbm],
        out_specs=(vmem, vmem),
        scratch_shapes=[
            pltpu.SMEM((1, entries), jnp.int32),
            pltpu.VMEM((row_count, col_count, *block), f32),
            pltpu.VMEM((rows, row_count * col_count, *block), f32),
            pltpu.VMEM((col_count, ancestors, *block), bf16),
            pltpu.VMEM((col_count, ancestors, *block), bf16),
            pltpu.VMEM((entries, *block), f32),
            pltpu.VMEM(block, f32),
            pltpu.VMEM((2, groups, entries, *block), f32),
            pltpu.SMEM((2 * groups, entries), jnp.int32),
            pltpu.VMEM((per_row, width, col_count * width), bf16),
            pltpu.VMEM((per_row, width, col_count * width), bf16),
            pltpu.VMEM((2, groups, col_count, *block), f32),
            pltpu.VMEM((row_count, *block), f32),
            pltpu.VMEM(block, f32),
            pltpu.VMEM((rows, *block), f32),
            dma((half, row_count * col_count)),
            dma((half, row_count * col_count)),
            dma((rows, row_count * col_count)),
            dma((2, groups, entries)),
            dma((entries,)),
            dma((groups, entries)),
            dma((groups, entries)),
            dma((groups, entries)),
            dma((4, groups)),
            dma((2, groups)),
            dma((2, groups, col_count)),
            dma((per_row, col_count)),
            dma((rows,)),
            dma((rows,)),
            dma((4,)),
        ],
        compiler_params=pltpu.CompilerParams(
            collective_id=0, has_side_effects=True, vmem_limit_bytes=48 * 1024 * 1024
        ),
    )(*(pltpu.with_memory_space_constraint(v, pltpu.HBM) for v in (sigma_anc, panel_u, structure, diag_inv)))


def solution(mesh):
    placed = (
        P("row", "col", None, None),
        P("col", None, None, None),
        P("col", None),
        P("col", None, None),
    )
    return jax.shard_map(
        local,
        mesh=mesh,
        in_specs=placed,
        out_specs=(P("col", "row", None, None), P("col", None, None)),
        check_vma=False,
    )
```

```python
import functools

import jax
import jax.numpy as jnp
from jax import lax
from jax.experimental import pallas as pl
from jax.experimental.pallas import tpu as pltpu
from jax.sharding import PartitionSpec as P

MESH = pl.DeviceIdType.MESH
HIGHEST = lax.Precision.HIGHEST
LAG = 3


def split(x):
    high = x.astype(jnp.bfloat16)
    return high, (x - high.astype(jnp.float32)).astype(jnp.bfloat16)


def dot(a, b):
    return jnp.dot(a, b, preferred_element_type=jnp.float32)


def dot_t(a, b):
    return lax.dot_general(
        a, b, (((0,), (0,)), ((), ())), precision=HIGHEST, preferred_element_type=jnp.float32
    )


def bend(plane):
    return lax.rem((plane + 1) // 2, 2)


def kernel(
    planes,
    rows,
    sigma_ref,
    u_ref,
    s_hbm,
    inv_ref,
    panel_ref,
    diag_ref,
    s_ref,
    own,
    raw,
    st_hi,
    st_lo,
    uown,
    iown,
    ubuf,
    sbuf,
    wt_hi,
    wt_lo,
    yout,
    yin,
    share,
    shares,
    x_send,
    c_send,
    s_recv,
    own_send,
    own_recv,
    a_send,
    o_send,
    a_recv,
    b_send,
    b_recv,
    n_send,
    n_recv,
    y_send,
    y_recv,
    d_send,
    d_recv,
    load,
):
    row_count, col_count, width = sigma_ref.shape[0], sigma_ref.shape[1], sigma_ref.shape[2]
    entries, groups = u_ref.shape[1], planes // rows
    half = rows // 2
    pack = 2 - entries % 2
    per_row = row_count // col_count
    col, row = lax.axis_index("col"), lax.axis_index("row")
    z, y = col // 2, lax.rem(col, 2)
    core = lax.rem(row, 2)
    mate, side = row + 1 - 2 * core, col + 1 - 2 * y

    def dev(c, r=None):
        return {"col": c, "row": row if r is None else r}

    depth = planes // 2
    upper = z // depth
    even = lax.rem(row // half + upper + y + 1, 2)

    def plane_of(i, e):
        odd = jnp.where(e == 0, even, 1 - even)
        return rows * i + jnp.where(core == 0, 3 * odd, 2 - odd)

    def node_col(i, e):
        return plane_of(i, e) * 2 + jnp.where(e == 0, y, 1 - y)

    def worker(other):
        return half * lax.rem(y + z + other // depth + 1, 2) + bend(z)

    crosses = jnp.logical_and(bend(z) == core, lax.rem(row // half + y + z + 1, 2) != upper)
    gate = jnp.where(upper == 0, depth, depth - 1)
    at_gate = z == jnp.where(upper == 0, depth - 1, depth)
    has_up = jnp.logical_and(z + 1 < planes, (z + 1) // depth == upper)
    has_down = jnp.logical_and(z > 0, (z + planes - 1) // depth - 2 == upper)

    def ways(i):
        source = plane_of(i, 0)
        within = source // depth == upper
        rises = jnp.where(within, z >= source, upper == 1)
        falls = jnp.where(within, z <= source, upper == 0)
        return jnp.logical_and(has_up, rises), jnp.logical_and(has_down, falls)

    home = col // per_row
    slot = z // rows

    barrier = pltpu.get_barrier_semaphore()

    def greet(where):
        pl.semaphore_signal(barrier, inc=1, device_id=where, device_id_type=MESH)

    local_sigma = pltpu.make_async_copy(sigma_ref, own, load.at[0])
    local_u = pltpu.make_async_copy(u_ref.at[0], uown, load.at[1])
    local_inv = pltpu.make_async_copy(inv_ref.at[0], iown, load.at[2])
    expected = jnp.int32(rows)
    number = lambda flag: flag.astype(jnp.int32)
    greet(dev(side))
    for o in range(1, rows):
        greet(dev(col, lax.rem(row + o, rows)))
    pl.when(has_up)(lambda: greet(dev(col + 2)))
    pl.when(has_down)(lambda: greet(dev(col - 2)))
    for i in range(groups):
        other = jnp.logical_and(at_gate, plane_of(i, 0) // depth != upper)
        pl.when(other)(lambda: greet(dev(node_col(i, 0))))
    expected += number(has_up) + number(has_down) + number(crosses)
    local_s = pltpu.make_async_copy(s_hbm, s_ref, load.at[3])
    local_s.start()
    local_u.start()
    local_sigma.start()
    local_inv.start()
    pl.semaphore_wait(barrier, expected)
    local_s.wait()

    def a_copy(i, n, way, source):
        return pltpu.make_async_remote_copy(
            source,
            ubuf.at[0, i, n],
            a_send.at[way, i, n],
            a_recv.at[i, n],
            dev(col + 2 - 4 * way),
            MESH,
        )

    def o_copy(n):
        return pltpu.make_async_remote_copy(
            u_ref.at[0, n], ubuf.at[0, slot, n], o_send.at[n], a_recv.at[slot, n], dev(gate * 2 + y), MESH
        )

    def b_copy(i, n, source):
        return pltpu.make_async_remote_copy(
            source, ubuf.at[1, i, n], b_send.at[i, n], b_recv.at[i, n], dev(side), MESH
        )

    def arrival(e, i, n, sems):
        mine = ubuf.at[e, i, n]
        return pltpu.make_async_remote_copy(mine, mine, b_send.at[i, n], sems.at[i, n], dev(side), MESH)

    def pass_on(i, n, source):
        for way, flag in enumerate(ways(i)):
            pl.when(flag)(a_copy(i, n, way, source).start)
        b_copy(i, n, source).start()

    def n_copies(i, source):
        def to(lane, e, where):
            return pltpu.make_async_remote_copy(
                source, sbuf.at[pl.ds(e * groups + i, 1)], n_send.at[lane, i], n_recv.at[e, i], dev(where), MESH
            )

        rises, falls = ways(i)
        return (rises, to(0, 0, col + 2)), (falls, to(1, 0, col - 2)), (True, to(2, 1, side))

    def n_cross():
        return pltpu.make_async_remote_copy(
            s_ref, sbuf.at[pl.ds(slot, 1)], n_send.at[3, 0], n_recv.at[0, slot], dev(gate * 2 + y), MESH
        )

    def n_arrival(e, i):
        mine = sbuf.at[pl.ds(e * groups + i, 1)]
        return pltpu.make_async_remote_copy(mine, mine, n_send.at[2, i], n_recv.at[e, i], dev(side), MESH)

    def x_copy(o, c):
        return pltpu.make_async_remote_copy(
            sigma_ref.at[lax.rem(c, row_count), c // row_count],
            raw.at[row, c],
            x_send.at[o, c],
            s_recv.at[row, c],
            dev(col, lax.rem(row + 2 * o, rows)),
            MESH,
        )

    def own_copy(q):
        return pltpu.make_async_remote_copy(
            sigma_ref.at[:, q],
            raw.at[row, pl.ds(q * row_count, row_count)],
            own_send.at[q],
            own_recv.at[q],
            dev(col, mate),
            MESH,
        )

    def own_arrival(q):
        mine = raw.at[mate, pl.ds(q * row_count, row_count)]
        return pltpu.make_async_remote_copy(
            mine, mine, own_send.at[q], own_recv.at[q], dev(col, mate), MESH
        )

    def c_copy(o, c):
        r = lax.rem(row + 2 * o, rows)
        return pltpu.make_async_remote_copy(
            raw.at[r, c], raw.at[r, c], c_send.at[o, c], s_recv.at[r, c], dev(col, mate), MESH
        )

    def s_arrival(r, c):
        return pltpu.make_async_remote_copy(
            raw.at[r, c], raw.at[r, c], c_send.at[0, c], s_recv.at[r, c], dev(col, mate), MESH
        )

    blocks = row_count * col_count

    def start_u():
        @pl.when(crosses)
        def _():
            n_cross().start()

            @pl.loop(0, entries)
            def _(n):
                o_copy(n).start()

        for i in range(groups):

            @pl.when(plane_of(i, 0) == z)
            def _():
                for flag, copy in n_copies(i, s_ref):
                    pl.when(flag)(copy.start)

                @pl.loop(0, entries)
                def _(n):
                    pass_on(i, n, u_ref.at[0, n])

    @pl.loop(0, blocks)
    def _(c):
        for o in range(1, half):
            x_copy(o, c).start()

    start_u()

    for q in range(col_count):
        own_copy(q).start()

    def member(b):
        found, where = jnp.int32(0), jnp.int32(0)
        for k in range(entries):
            hit = s_ref[0, k] == b
            found, where = jnp.where(hit, 1, found), jnp.where(hit, k, where)
        return found.astype(jnp.float32), where

    def keep(r, c, source):
        high, low = split(source[...].T)
        st_hi[c // row_count, r * row_count + lax.rem(c, row_count)] = high
        st_lo[c // row_count, r * row_count + lax.rem(c, row_count)] = low

    local_u.wait()
    for i in range(groups):

        @pl.when(plane_of(i, 0) == z)
        def _():
            ubuf[0, i] = uown[...]
            for k in range(entries):
                sbuf[i, k] = s_ref[0, k]

    local_sigma.wait()

    @pl.loop(0, blocks)
    def _(c):
        keep(row, c, own.at[lax.rem(c, row_count), c // row_count])

    def s_mated(c):
        for o in range(1, half):
            r = lax.rem(mate + 2 * o, rows)
            s_arrival(r, c).wait_recv()
            keep(r, c, raw.at[r, c])

    def s_forward(c):
        for o in range(1, half):
            r = lax.rem(row + 2 * o, rows)
            s_arrival(r, c).wait_recv()
            c_copy(o, c).start()
            keep(r, c, raw.at[r, c])
        pl.when(lax.rem(c, row_count) == 0)(lambda: own_arrival(c // row_count).wait_recv())
        keep(mate, c, raw.at[mate, c])
        pl.when(c > 0)(lambda: s_mated(c - 1))

    def self_out(i, e):
        return jnp.logical_and(node_col(i, e) == col, home == row)

    def y_copy(i, e, q):
        return pltpu.make_async_remote_copy(
            yout.at[e, i, q],
            yin.at[lax.rem(col, per_row) * col_count + q],
            y_send.at[e, i, q],
            y_recv.at[lax.rem(col, per_row), q],
            dev(node_col(i, e), home),
            MESH,
        )

    def finish(e, i, q):
        def term(k, total):
            picks = [k * pack + p for p in range(pack)]
            high, low = split(jnp.concatenate([ubuf[e, i, p] for p in picks], axis=0))
            near = [sbuf[e * groups + i, p] for p in picks]
            st_h = jnp.concatenate([st_hi[q, b] for b in near], axis=1)
            st_l = jnp.concatenate([st_lo[q, b] for b in near], axis=1)
            both = dot(st_h, jnp.concatenate([high, low], axis=1))
            return total + (both[:, :width] + (both[:, width:] + dot(st_l, high)))

        yout[e, i, q] = lax.fori_loop(
            0,
            entries // pack,
            term,
            jnp.zeros((width, width), jnp.float32),
            unroll=min(entries // pack, 4),
        )

        @pl.when(jnp.logical_not(self_out(i, e)))
        def _():
            y_copy(i, e, q).start()

        @pl.when(self_out(i, e))
        def _():
            yin[lax.rem(col, per_row) * col_count + q] = yout[e, i, q]

    def pace(n):
        return n * blocks // (2 * entries) + 1

    def late(i):
        first = jnp.where(upper == 0, depth - 1, depth)
        return jnp.where(plane_of(i, 0) // depth == upper, 0, LAG * jnp.abs(z - first))

    steps = entries + LAG * (depth - 1)
    ready = [
        next(t for t in range(3 * entries) if pace(t) >= min((q + 1) * row_count + 1, blocks))
        for q in range(col_count)
    ]
    steps = max(steps, ready[-1] + 1)

    @pl.loop(0, steps)
    def _(t):
        for i in range(groups):
            n = t - late(i)

            @pl.when(jnp.logical_and(plane_of(i, 0) != z, jnp.logical_and(n >= 0, n < entries)))
            def _():
                @pl.when(n == 0)
                def _():
                    n_arrival(0, i).wait_recv()
                    for flag, copy in n_copies(i, sbuf.at[pl.ds(i, 1)]):
                        pl.when(flag)(copy.start)

                arrival(0, i, n, a_recv).wait_recv()
                pass_on(i, n, ubuf.at[0, i, n])

        before = jnp.where(t == 0, 0, pace(t - 1))
        fresh = jnp.logical_and(pace(t) > before, before < blocks)
        pl.when(fresh)(lambda: s_forward(before))
        for i in range(groups):
            for q in range(col_count - 1):
                when = jnp.maximum(ready[q], late(i) + entries - 1)
                pl.when(t == when)(functools.partial(finish, 0, i, q))

    def y_from(i):
        return row * per_row + i

    def y_arrival(i, q):
        mine = yin.at[i * col_count + q]
        return pltpu.make_async_remote_copy(
            mine, mine, y_send.at[0, 0, q], y_recv.at[i, q], dev(side), MESH
        )

    s_mated(blocks - 1)
    for i in range(groups):
        finish(0, i, col_count - 1)
    for i in range(groups):
        n_arrival(1, i).wait_recv()
        for n in range(entries):
            arrival(1, i, n, b_recv).wait_recv()
        for q in range(col_count):
            finish(1, i, q)

    row_start = row * row_count
    found = []
    for a in range(row_count):
        here, where = member(row_start + a)
        found.append(here)
        high, low = split((uown[where] * here).T)
        lanes = slice(a % col_count * width, (a % col_count + 1) * width)
        wt_hi[a // col_count, :, lanes] = high
        wt_lo[a // col_count, :, lanes] = low

    total = jnp.zeros((width, width), jnp.float32)
    for i in range(per_row):
        other = y_from(i)

        @pl.when(jnp.logical_or(other != col, worker(other // 2) != row))
        def _():
            for q in range(col_count):
                y_arrival(i, q).wait_recv()

        panels = []
        for q in range(col_count):
            a = i * col_count + q
            panels.append(-yin[a] * found[a])
            panel_ref[0, a] = panels[q]
        high, low = split(jnp.concatenate(panels, axis=0))
        both = dot(wt_hi[i], jnp.concatenate([high, low], axis=1))
        total += both[:, :width] + (both[:, width:] + dot(wt_lo[i], high))
    share[...] = total

    def d_copy(o):
        return pltpu.make_async_remote_copy(
            share, shares.at[row], d_send.at[o], d_recv.at[row], dev(col, lax.rem(row + o, rows)), MESH
        )

    def d_arrival(r):
        mine = shares.at[r]
        return pltpu.make_async_remote_copy(mine, mine, d_send.at[0], d_recv.at[r], dev(side), MESH)

    for o in range(1, rows):
        d_copy(o).start()

    local_inv.wait()
    inv = iown[...]
    diag_ref[0] = dot_t(inv, inv)

    for q in range(col_count):
        own_copy(q).wait_send()
    @pl.loop(0, blocks)
    def _(c):
        for o in range(1, half):
            x_copy(o, c).wait_send()
            c_copy(o, c).wait_send()

    @pl.when(crosses)
    def _():
        n_cross().wait_send()

        @pl.loop(0, entries)
        def _(n):
            o_copy(n).wait_send()

    for i in range(groups):
        for flag, copy in n_copies(i, s_ref):
            pl.when(flag)(copy.wait_send)
        for e in range(2):
            for q in range(col_count):
                pl.when(jnp.logical_not(self_out(i, e)))(y_copy(i, e, q).wait_send)

        @pl.loop(0, entries)
        def _(n):
            for way, flag in enumerate(ways(i)):
                pl.when(flag)(a_copy(i, n, way, u_ref.at[0, n]).wait_send)
            b_copy(i, n, u_ref.at[0, n]).wait_send()

    shares[row] = total
    total = -diag_ref[0]
    for r in range(rows):
        pl.when(row != r)(d_arrival(r).wait_recv)
        total += shares[r]
    diag_ref[0] = -total
    for o in range(1, rows):
        d_copy(o).wait_send()


def deliver(panel_ref, diag_ref, panel_out, diag_out, sems):
    copies = [
        pltpu.make_async_copy(panel_ref, panel_out, sems.at[0]),
        pltpu.make_async_copy(diag_ref, diag_out, sems.at[1]),
    ]
    for copy in copies:
        copy.start()
    for copy in copies:
        copy.wait()


def local(sigma_anc, panel_u, structure, diag_inv):
    row_count, col_count, width = sigma_anc.shape[0], sigma_anc.shape[1], sigma_anc.shape[2]
    entries = panel_u.shape[1]
    cols, rows = lax.axis_size("col"), lax.axis_size("row")
    planes, half = cols // 2, rows // 2
    groups = planes // rows
    per_row = row_count // col_count
    ancestors = rows * row_count
    block = (width, width)
    f32, bf16 = jnp.float32, jnp.bfloat16
    vmem, hbm = pl.BlockSpec(memory_space=pltpu.VMEM), pl.BlockSpec(memory_space=pl.ANY)
    dma = pltpu.SemaphoreType.DMA
    outs = pl.pallas_call(
        functools.partial(kernel, planes, rows),
        out_shape=(
            jax.ShapeDtypeStruct((1, row_count, *block), f32),
            jax.ShapeDtypeStruct((1, *block), f32),
        ),
        in_specs=[hbm, hbm, hbm, hbm],
        out_specs=(vmem, vmem),
        scratch_shapes=[
            pltpu.SMEM((1, entries), jnp.int32),
            pltpu.VMEM((row_count, col_count, *block), f32),
            pltpu.VMEM((rows, row_count * col_count, *block), f32),
            pltpu.VMEM((col_count, ancestors, *block), bf16),
            pltpu.VMEM((col_count, ancestors, *block), bf16),
            pltpu.VMEM((entries, *block), f32),
            pltpu.VMEM(block, f32),
            pltpu.VMEM((2, groups, entries, *block), f32),
            pltpu.SMEM((2 * groups, entries), jnp.int32),
            pltpu.VMEM((per_row, width, col_count * width), bf16),
            pltpu.VMEM((per_row, width, col_count * width), bf16),
            pltpu.VMEM((2, groups, col_count, *block), f32),
            pltpu.VMEM((row_count, *block), f32),
            pltpu.VMEM(block, f32),
            pltpu.VMEM((rows, *block), f32),
            dma((half, row_count * col_count)),
            dma((half, row_count * col_count)),
            dma((rows, row_count * col_count)),
            dma((col_count,)),
            dma((col_count,)),
            dma((2, groups, entries)),
            dma((entries,)),
            dma((groups, entries)),
            dma((groups, entries)),
            dma((groups, entries)),
            dma((4, groups)),
            dma((2, groups)),
            dma((2, groups, col_count)),
            dma((per_row, col_count)),
            dma((rows,)),
            dma((rows,)),
            dma((4,)),
        ],
        compiler_params=pltpu.CompilerParams(
            collective_id=0, has_side_effects=True, vmem_limit_bytes=48 * 1024 * 1024
        ),
    )(*(pltpu.with_memory_space_constraint(v, pltpu.HBM) for v in (sigma_anc, panel_u, structure, diag_inv)))
    return pl.pallas_call(
        deliver,
        out_shape=tuple(jax.ShapeDtypeStruct(v.shape, v.dtype) for v in outs),
        in_specs=[vmem, vmem],
        out_specs=(pl.BlockSpec(memory_space=pltpu.HBM),) * 2,
        scratch_shapes=[dma((2,))],
    )(*(pltpu.with_memory_space_constraint(v, pltpu.VMEM) for v in outs))


def solution(mesh):
    placed = (
        P("row", "col", None, None),
        P("col", None, None, None),
        P("col", None),
        P("col", None, None),
    )
    return jax.shard_map(
        local,
        mesh=mesh,
        in_specs=placed,
        out_specs=(P("col", "row", None, None), P("col", None, None)),
        check_vma=False,
    )
```
